256 devices in a mesh: gx: 16 (over x_lo, z), gy: 4 (over y), gz: 4 (over x_hi, core).
Axes of the slice: x: 4 (x_hi: 2, x_lo: 2; x = x_hi * 2 + x_lo), y: 4, z: 8, core: 2. Of those that a mesh axis runs over, the one named last changes fastest.
Arguments:
- concentration: float32 [256, 512, 1024], P('gz', 'gx', 'gy'), may hold values from -6 to 6
- pit_mask: int32 [256, 512, 1024], P('gz', 'gx', 'gy'), may hold values 0 or 1
- phase_ids: int32 [256, 512, 1024], P('gz', 'gx', 'gy'), may hold values from 0 to 3
- bond_offsets: int32 [28, 2], replicated, may hold values from -3 to 3, as said below
- damage: int32 [256, 512, 1024], P('gz', 'gx', 'gy'), may hold values 0 or 1
- bond_weight: float32 [28], replicated, may hold values from 0.25 to 1
- phase_diffusivity: float32 [4], replicated, may hold values from 0.25 to 1
- phase_rate: float32 [4], replicated, may hold values from 0.5 to 2
Outputs:
- updated: float32 [256, 512, 1024], P('gz', 'gx', 'gy')
The draws below stay inside these ranges and needn't reach their ends.
Inputs may be any that keep to these rules, and one draw needn't show every extreme that they name: `bond_offsets`: each row is a distinct nonzero lateral offset; the four offsets (3, 0), (-3, 0), (0, 3), (0, -3) are always among them.
All inputs are finite; a program needn't handle non-finite values. No bound on the sum of `pit_mask` or of `damage` on one device may be relied on, other than what follows from the above.
Results may differ from the reference program's by a relative error of at most 0.0006.
Values sent between devices are 32-bit elements; how exact they have to be, the bound alone decides.
No kernel may reach another device: no remote copies, remote signals or barrier semaphores. Data moves between devices by JAX's collectives and lax.ppermute only.
A program may use at most 128 MiB of HBM per device.

```python
import math
import jax
import jax.numpy as jnp
import numpy as np
from jax import lax

CZ = 64
BONDS = 28
NPHASE = 4
SUBSTEPS = 2
NX = 512
NY = 1024
NZ = 256


def offset_table():
    forced = [(3, 0), (-3, 0), (0, 3), (0, -3)]
    others = []
    for first in range(-3, 4):
        for second in range(-3, 4):
            if (first, second) != (0, 0) and (first, second) not in forced:
                others.append((first, second))
    return (np.array(forced, np.int32), np.array(others, np.int32))


def draw_bond_offsets(key, part):
    forced, others = offset_table()
    picker = jax.random.fold_in(key, 7)
    chosen = jnp.asarray(others)[jax.random.permutation(picker, others.shape[0])[:24]]
    table = jnp.concatenate([jnp.asarray(forced), chosen], axis=0)
    order = jax.random.permutation(jax.random.fold_in(key, 9), 28)
    return table[order].astype(jnp.int32)


def draw_concentration(key, part):
    base = jax.random.fold_in(key, 11)
    column_key, noise_key = jax.random.split(base)
    column = jax.random.normal(column_key, (1, NX, NY), jnp.float32)
    noise = jax.random.normal(noise_key, (NZ, NX, NY), jnp.float32)
    values = column + 0.5 * noise
    return jnp.clip(values, -6.0, 6.0).astype(jnp.float32)


def place_ends(result, key, least, top_value):
    dims = result.shape
    index_at = [jax.random.randint(jax.random.fold_in(key, axis), (), 0, dims[axis]) for axis in range(len(dims))]
    result = result.at[tuple(index_at)].set(least)
    longest = dims.index(max(dims))
    index_at[longest] = (index_at[longest] + 1) % dims[longest]
    return result.at[tuple(index_at)].set(top_value)


def setup_inputs(seed: int = 0) -> dict:
    arg_keys = jax.random.split(jax.random.key(seed), 9)
    return {
        "concentration": draw_concentration(jax.random.fold_in(arg_keys[8], 71), 0),
        "pit_mask": place_ends((jax.random.randint(arg_keys[1], (NZ, NX, NY), 0, 8) < 1).astype(jnp.int32), jax.random.fold_in(arg_keys[1], 1), 0, 1),
        "phase_ids": place_ends(jax.random.randint(arg_keys[2], (NZ, NX, NY), 0, NPHASE), jax.random.fold_in(arg_keys[2], 1), 0, NPHASE - 1).astype(jnp.int32),
        "bond_offsets": draw_bond_offsets(jax.random.fold_in(arg_keys[8], 71), 0),
        "damage": place_ends((jax.random.randint(arg_keys[4], (NZ, NX, NY), 0, 4) < 1).astype(jnp.int32), jax.random.fold_in(arg_keys[4], 1), 0, 1),
        "bond_weight": jnp.clip(jnp.exp(jax.random.uniform(arg_keys[5], (BONDS,), jnp.float32, math.log(0.25), math.log(1.0))), 0.25, 1.0),
        "phase_diffusivity": jnp.clip(jnp.exp(jax.random.uniform(arg_keys[6], (NPHASE,), jnp.float32, math.log(0.25), math.log(1.0))), 0.25, 1.0),
        "phase_rate": jnp.clip(jnp.exp(jax.random.uniform(arg_keys[7], (NPHASE,), jnp.float32, math.log(0.5), math.log(2.0))), 0.5, 2.0),
    }


lateral_step = 0.02
dissolve_step = 0.25

def phase_lookup(phase_ids, table):
    total = jnp.zeros(phase_ids.shape, jnp.float32)
    for phase in range(NPHASE):
        total = total + jnp.where(phase_ids == phase, table[phase], jnp.float32(0.0))
    return total

def reference(concentration, pit_mask, phase_ids, bond_offsets, damage, bond_weight, phase_diffusivity, phase_rate):
    mobility = phase_lookup(phase_ids, phase_diffusivity) * (1.0 + 0.5 * damage.astype(jnp.float32))
    source = phase_lookup(phase_ids, phase_rate) * pit_mask.astype(jnp.float32)
    field = concentration
    for substep in range(SUBSTEPS):
        current = field

        def add_bond(bond, flux):
            moved = jnp.roll(current, (-bond_offsets[bond, 0], -bond_offsets[bond, 1]), axis=(1, 2))
            return flux + bond_weight[bond] * (moved - current)
        flux = lax.fori_loop(0, BONDS, add_bond, jnp.zeros_like(current))
        field = current + lateral_step * mobility * flux + dissolve_step * source * (1.0 - current)
    stiff = 3.0 * CZ * CZ
    lower = jnp.full((NZ,), -stiff, field.dtype).at[0].set(0.0)
    upper = jnp.full((NZ,), -stiff, field.dtype).at[NZ - 1].set(0.0)
    middle = jnp.full((NZ,), 1.0 + 2.0 * stiff, field.dtype)
    middle = middle.at[0].set(1.0 + stiff).at[NZ - 1].set(1.0 + stiff)
    flat = field.reshape(NZ, NX * NY)
    solved = lax.linalg.tridiagonal_solve(lower, middle, upper, flat)
    return (2.0 * solved - flat).reshape(NZ, NX, NY)
```

```python
import functools

import jax
import jax.numpy as jnp
import numpy as np
from jax import lax
from jax.experimental import pallas as pl
from jax.experimental.pallas import tpu as pltpu
from jax.sharding import PartitionSpec as P

DZ, DX, DY = 64, 32, 256
BONDS = 28
INNER = DX - 6
f32, bf16 = jnp.float32, jnp.bfloat16
lateral_step = 0.02
dissolve_step = 0.25

VMEM = pl.BlockSpec(memory_space=pltpu.VMEM)
SMEM = pl.BlockSpec(memory_space=pltpu.SMEM)
HBM = pl.BlockSpec(memory_space=pl.ANY)


def call(kernel, name, out_shape, in_specs, out_specs, scratch=(), aliases=None, flops=0, nbytes=1 << 20):
    return pl.pallas_call(
        kernel,
        name=name,
        out_shape=out_shape,
        in_specs=in_specs,
        out_specs=out_specs,
        scratch_shapes=list(scratch),
        input_output_aliases=aliases or {},
        cost_estimate=pl.CostEstimate(flops=flops, bytes_accessed=nbytes, transcendentals=0),
        compiler_params=pltpu.CompilerParams(vmem_limit_bytes=48 << 20),
    )


def struct(*dims, dtype=f32):
    return jax.ShapeDtypeStruct(dims, dtype)


def lanes():
    return lax.broadcasted_iota(jnp.int32, (DZ, 128), 1)


def add_to_pack(pack, row, x):
    slot = 8 * (x % 16)
    lane = lanes()
    last = pltpu.roll(row[:, 128:], (slot + 3) % 128, 1)
    first = pltpu.roll(row[:, :128], (slot + 4) % 128, 1)
    pack = jnp.where((lane >= slot) & (lane < slot + 3), last, pack)
    return jnp.where((lane >= slot + 4) & (lane < slot + 7), first, pack)


def split(value):
    high = value.astype(bf16)
    return high, (value - high.astype(f32)).astype(bf16)


def edge_window(before, after, x):
    slot = 8 * ((x + 13) % 16)
    lane = lanes()
    window = pltpu.roll(jnp.where(lane >= slot, before, after), (128 - slot) % 128, 1)
    high = window.astype(bf16).astype(f32)
    low = pltpu.roll(window - high, 64, 1)
    return jnp.concatenate([jnp.where(lane < 64, high, low).astype(bf16), high.astype(bf16)], axis=1)


def weights_kernel(offsets, weight, w_ref, table):
    for place in range(49):
        table[place] = jnp.float32(0.0)
    for bond in range(BONDS):
        place = (offsets[2 * bond] + 3) * 7 + offsets[2 * bond + 1] + 3
        table[place] = table[place] + weight[bond]
    diff = lax.broadcasted_iota(jnp.int32, (DY, DY), 0) - lax.broadcasted_iota(jnp.int32, (DY, DY), 1) + 3

    @pl.loop(0, 7)
    def _(first):
        band = jnp.zeros((DY, DY), f32)
        for second in range(7):
            band = jnp.where(diff == second, table[first * 7 + second], band)
        w_ref[first], w_ref[7 + first] = split(band)

    lane = lax.broadcasted_iota(jnp.int32, (128, DY), 0)
    column = lax.broadcasted_iota(jnp.int32, (128, DY), 1)
    place = lane % 8
    which = jnp.where(place < 4, place - column, 255 + place - column)
    which = jnp.where((place == 3) | (place == 7), -1, which)
    which = jnp.where((which >= 0) & (which < 7), which, -100) + 7 * ((lane % 64) // 8)
    edge = jnp.zeros((128, DY), f32)
    for place in range(49):
        edge = jnp.where(which == place, table[place], edge)
    high, low = split(edge)
    w_ref[14, :128, :] = high
    w_ref[14, 128:, :] = jnp.where(lane < 64, low.astype(f32), 0.0).astype(bf16)


def right_side(w_ref):
    bands = [w_ref[a] for a in range(7)]
    return jnp.concatenate(bands + bands + [w_ref[7 + a] for a in range(7)] + [w_ref[14]], axis=0)


def flat(value):
    return value.reshape(value.shape[0] * DZ, DY)


def total_weight(weight):
    total = weight[0]
    for bond in range(1, BONDS):
        total = total + weight[bond]
    return total


def stepped(center, flux, pit, phase, damage, diffusivity, rate, weight_sum):
    def look(table, scale):
        value = jnp.where(phase == 0, table[0] * scale, table[1] * scale)
        return jnp.where(phase < 2, value, jnp.where(phase == 2, table[2] * scale, table[3] * scale))

    mobility = look(diffusivity, lateral_step) * (1.0 + 0.5 * damage.astype(f32))
    source = look(rate, dissolve_step) * pit.astype(f32)
    return center + mobility * (flux - weight_sum * center) + source * (1.0 - center)


def first_kernel(conc, field, pack, up, down, buf, sem, out_sem):
    for x in range(DX):
        pltpu.make_async_copy(conc.at[:, x, :], buf.at[x], sem.at[x // 8]).start()
    for group in range(4):
        for x in range(8 * group, 8 * group + 8):
            pltpu.make_async_copy(conc.at[:, x, :], buf.at[x], sem.at[group]).wait()
        part = pl.ds(8 * group, 8)
        pltpu.make_async_copy(buf.at[part], field.at[part], out_sem.at[group]).start()
        if group % 2 == 0:
            packed = jnp.zeros((DZ, 128), f32)
        for x in range(8 * group, 8 * group + 8):
            packed = add_to_pack(packed, buf[x], x)
        if group % 2:
            pack[group // 2] = packed
    for row in range(3):
        for half in range(2):
            down[2 * row + half] = buf[row, :, 128 * half : 128 * half + 128]
            up[2 * row + half] = buf[DX - 3 + row, :, 128 * half : 128 * half + 128]
    down[6] = jnp.zeros((DZ, 128), f32)
    up[6] = jnp.zeros((DZ, 128), f32)
    for group in range(4):
        part = pl.ds(8 * group, 8)
        pltpu.make_async_copy(buf.at[part], field.at[part], out_sem.at[group]).wait()


def join_kernel(left, right, up_in, down_in, halo, up, down, sem):
    lane = lanes()
    for group in range(2):
        halo[group] = jnp.where(lane % 8 < 4, left[group], right[group])
    copies = [
        pltpu.make_async_copy(halo.at[1], up.at[6], sem.at[0]),
        pltpu.make_async_copy(halo.at[0], down.at[6], sem.at[1]),
    ]
    for copy in copies:
        copy.start()
    for copy in copies:
        copy.wait()


CHUNK = INNER // 2


def inner_kernel(
    last, field, halo, pit, phase, damage, w_ref, weight, diffusivity, rate, sums, out, extra,
    buf, high, low, edges, pv, hv, dv, flux, res, sem, int_sem, out_sem,
):
    def field_copy(group):
        part = pl.ds(8 * group, 8)
        return pltpu.make_async_copy(field.at[part], buf.at[part], sem.at[group])

    def int_copies(chunk):
        for row in range(CHUNK * chunk, CHUNK * chunk + CHUNK):
            for source, target in ((pit, pv), (phase, hv), (damage, dv)):
                yield pltpu.make_async_copy(source.at[:, 3 + row, :], target.at[row], int_sem.at[chunk])

    for group in range(4):
        field_copy(group).start()
    for chunk in range(2):
        for copy in int_copies(chunk):
            copy.start()
    for x in range(3, DX - 3):
        group = (x + 13) // 16 - 1
        edges[x - 3] = edge_window(halo[group], halo[min(group + 1, 1)], x)
    for group in range(4):
        field_copy(group).wait()

        @pl.loop(0, 8)
        def _(row):
            x = 8 * group + row
            high[x], low[x] = split(buf[x])

    weight_sum = total_weight(weight)

    for chunk in range(2):
        row = CHUNK * chunk

        def rows(ref, a):
            return flat(ref[row + a : row + a + CHUNK])

        left = [rows(high, a) for a in range(7)] + [rows(low, a) for a in range(7)]
        left = left + [rows(high, a) for a in range(7)] + [rows(edges, 0)]
        flux[...] = jnp.dot(
            jnp.concatenate(left, axis=1), right_side(w_ref), preferred_element_type=f32
        ).reshape(CHUNK, DZ, DY)
        for copy in int_copies(chunk):
            copy.wait()

        @pl.loop(0, CHUNK)
        def _(i):
            res[row + i] = stepped(
                buf[row + i + 3], flux[i], pv[row + i], hv[row + i], dv[row + i], diffusivity, rate, weight_sum
            )

        part = pl.ds(row, CHUNK)
        pltpu.make_async_copy(res.at[part], out.at[pl.ds(3 + row, CHUNK)], out_sem.at[chunk]).start()
    if last:
        extra[...] = jnp.zeros_like(extra)
        depth_sums(res, sums, extra, 3, INNER, 0)
    else:
        for group in range(2):
            packed = jnp.zeros((DZ, 128), f32)
            for x in range(max(3, 16 * group), min(DX - 3, 16 * group + 16)):
                packed = add_to_pack(packed, res[x - 3], x)
            extra[group] = packed
    for chunk in range(2):
        row = CHUNK * chunk
        pltpu.make_async_copy(
            res.at[pl.ds(row, CHUNK)], out.at[pl.ds(3 + row, CHUNK)], out_sem.at[chunk]
        ).wait()


def depth_sums(res, sums, extra, start, count, first):
    own = lax.axis_index("gz")
    below = jnp.zeros((count, DY), f32)
    above = jnp.zeros((count, DY), f32)
    for z in range(DZ):
        value = res[first : first + count, z, :]
        below = below + sums[own, z] * value
        above = above + sums[own, DZ + z] * value
    extra[0, start : start + count, :] = below
    extra[1, start : start + count, :] = above


def outer_kernel(
    last, field, halo, from_low, from_high, pit, phase, damage, w_ref, weight, diffusivity, rate, sums,
    out_in, extra_in, out, extra, *rest,
):
    if last:
        buf, high, low, edges, pv, hv, dv, res, sem, int_sem, out_sem = rest
    else:
        up, down, buf, high, low, edges, pv, hv, dv, res, sem, int_sem, out_sem = rest
    field_copies = [
        pltpu.make_async_copy(field.at[pl.ds(0, 6)], buf.at[pl.ds(3, 6)], sem.at[0]),
        pltpu.make_async_copy(field.at[pl.ds(DX - 6, 6)], buf.at[pl.ds(9, 6)], sem.at[1]),
    ]
    places = [0, 1, 2, DX - 3, DX - 2, DX - 1]
    int_copies = [
        pltpu.make_async_copy(source.at[:, x, :], target.at[row], int_sem.at[0])
        for row, x in enumerate(places)
        for source, target in ((pit, pv), (phase, hv), (damage, dv))
    ]
    for copy in field_copies + int_copies:
        copy.start()
    groups = [from_low[6], halo[0], halo[1], from_high[6]]
    for row, x in enumerate(places):
        group = (x + 13) // 16
        edges[row] = edge_window(groups[group], groups[min(group + 1, 3)], x)
    for row in range(3):
        for half in range(2):
            part = slice(128 * half, 128 * half + 128)
            buf[row, :, part] = from_low[2 * row + half]
            buf[15 + row, :, part] = from_high[2 * row + half]
    for copy in field_copies:
        copy.wait()

    @pl.loop(0, 18)
    def _(row):
        high[row], low[row] = split(buf[row])

    weight_sum = total_weight(weight)

    def rows(ref, a):
        return jnp.concatenate([flat(ref[a : a + 3]), flat(ref[9 + a : 12 + a])], axis=0)

    left = [rows(high, a) for a in range(7)] + [rows(low, a) for a in range(7)]
    left = left + [rows(high, a) for a in range(7)] + [flat(edges[...])]
    res[...] = jnp.dot(
        jnp.concatenate(left, axis=1), right_side(w_ref), preferred_element_type=f32
    ).reshape(6, DZ, DY)
    for copy in int_copies:
        copy.wait()

    for row in range(6):
        center = buf[3 + row] if row < 3 else buf[9 + row]
        res[row] = stepped(center, res[row], pv[row], hv[row], dv[row], diffusivity, rate, weight_sum)
    out_copies = [
        pltpu.make_async_copy(res.at[pl.ds(0, 3)], out.at[pl.ds(0, 3)], out_sem.at[0]),
        pltpu.make_async_copy(res.at[pl.ds(3, 3)], out.at[pl.ds(DX - 3, 3)], out_sem.at[1]),
    ]
    for copy in out_copies:
        copy.start()
    if last:
        extra[...] = extra_in[...]
        depth_sums(res, sums, extra, 0, 3, 0)
        depth_sums(res, sums, extra, DX - 3, 3, 3)
    else:
        packed = [extra_in[0], extra_in[1]]
        for row, x in enumerate(places):
            packed[x // 16] = add_to_pack(packed[x // 16], res[row], x)
        for group in range(2):
            extra[group] = packed[group]
        for row in range(3):
            for half in range(2):
                part = slice(128 * half, 128 * half + 128)
                down[2 * row + half] = res[row, :, part]
                up[2 * row + half] = res[3 + row, :, part]
        down[6] = jnp.zeros((DZ, 128), f32)
        up[6] = jnp.zeros((DZ, 128), f32)
    for copy in out_copies:
        copy.wait()


def depth_tables(blocks):
    stiff = 3.0 * DZ * DZ
    count = DZ * blocks
    diagonal = np.full(count, 1.0 + 2.0 * stiff)
    diagonal[0] = diagonal[-1] = 1.0 + stiff
    fore = diagonal.copy()
    for i in range(1, count):
        fore[i] = diagonal[i] - stiff * stiff / fore[i - 1]
    back = diagonal.copy()
    for i in range(count - 2, -1, -1):
        back[i] = diagonal[i] - stiff * stiff / back[i + 1]
    sums = np.zeros((blocks, 2 * DZ))
    solve = np.zeros((blocks, 2 * DZ + 2 * blocks))
    for block in range(blocks):
        start, end = block * DZ, block * DZ + DZ - 1
        for z in range(DZ):
            sums[block, z] = np.prod(stiff / fore[start + z : end])
            sums[block, DZ + z] = np.prod(stiff / back[start + 1 : start + z + 1])
            solve[block, z] = stiff / fore[start + z - 1] if start + z else 0.0
            solve[block, DZ + z] = 1.0 / fore[start + z]
        if block < blocks - 1:
            solve[block, 2 * DZ - 1] = 1.0 / (fore[end] - stiff * stiff / back[end + 1])
        for other in range(blocks):
            if other < block:
                solve[block, 2 * DZ + other] = np.prod(stiff / fore[other * DZ + DZ - 1 : start])
            if other > block:
                solve[block, 2 * DZ + blocks + other] = np.prod(stiff / back[end + 1 : other * DZ + 1])
    return jnp.asarray(sums, f32), jnp.asarray(solve, f32)


def depth_kernel(blocks, field, every, solve, out, buf, sweep, sem, out_sem):
    parts = [pl.ds(8 * group, 8) for group in range(4)]
    for group in range(4):
        pltpu.make_async_copy(field.at[parts[group]], buf.at[parts[group]], sem.at[group]).start()
    own = lax.axis_index("gz")
    stiff = 3.0 * DZ * DZ
    above = jnp.zeros((DX, DY), f32)
    below = jnp.zeros((DX, DY), f32)
    for block in range(blocks):
        above = above + solve[own, 2 * DZ + block] * every[block, 0]
        below = below + solve[own, 2 * DZ + blocks + block] * every[block, 1]
    for group in range(4):
        pltpu.make_async_copy(field.at[parts[group]], buf.at[parts[group]], sem.at[group]).wait()
    value = above
    for z in range(DZ):
        carried = value if z == 0 else solve[own, z] * value
        value = buf[:, z, :] + carried
        sweep[z] = value
    value = (value + below) * solve[own, 2 * DZ - 1]
    for z in range(DZ - 1, -1, -1):
        if z < DZ - 1:
            value = (sweep[z] + stiff * value) * solve[own, DZ + z]
        sweep[z] = 2.0 * value - buf[:, z, :]
        if z % 16 == 0:
            part = pl.ds(z, 16)
            pltpu.make_async_copy(sweep.at[part], out.at[part], out_sem.at[z // 16]).start()
    for z in range(0, DZ, 16):
        part = pl.ds(z, 16)
        pltpu.make_async_copy(sweep.at[part], out.at[part], out_sem.at[z // 16]).wait()


def shift(value, axis, step):
    count = lax.axis_size(axis)
    return lax.ppermute(value, axis, [(i, (i + step) % count) for i in range(count)])


def local(conc, pit, phase, offsets, damage, weight, diffusivity, rate):
    blocks = lax.axis_size("gz")
    sums, solve = depth_tables(blocks)
    sem = pltpu.SemaphoreType.DMA
    slab = struct(7, DZ, 128)
    whole = struct(DX, DZ, DY)
    field, pack, up, down = call(
        first_kernel, "first", (whole, struct(2, DZ, 128), slab, slab),
        [HBM], (HBM, VMEM, VMEM, VMEM),
        [pltpu.VMEM((DX, DZ, DY), f32), sem((4,)), sem((4,))], nbytes=4 << 20,
    )(conc)
    w = call(
        weights_kernel, "weights", struct(15, DY, DY, dtype=bf16), [SMEM, SMEM], VMEM, [pltpu.SMEM((64,), f32)],
    )(offsets.reshape(2 * BONDS), weight)
    for substep in range(2):
        last = substep == 1
        left, right = shift(pack, "gy", 1), shift(pack, "gy", -1)
        halo, up, down = call(
            join_kernel, "join", (struct(2, DZ, 128), slab, slab),
            [VMEM, VMEM, HBM, HBM], (VMEM, HBM, HBM), [sem((2,))], {2: 1, 3: 2},
        )(left, right, up, down)
        from_low, from_high = shift(up, "gx", 1), shift(down, "gx", -1)
        extra = struct(2, DX, DY) if last else struct(2, DZ, 128)
        out, more = call(
            functools.partial(inner_kernel, last), f"inner{substep}", (whole, extra),
            [HBM, VMEM, HBM, HBM, HBM, VMEM, SMEM, SMEM, SMEM, SMEM], (HBM, VMEM),
            [
                pltpu.VMEM((DX, DZ, DY), f32), pltpu.VMEM((DX, DZ, DY), bf16), pltpu.VMEM((DX, DZ, DY), bf16),
                pltpu.VMEM((INNER, DZ, DY), bf16),
                pltpu.VMEM((INNER, DZ, DY), jnp.int32), pltpu.VMEM((INNER, DZ, DY), jnp.int32),
                pltpu.VMEM((INNER, DZ, DY), jnp.int32),
                pltpu.VMEM((CHUNK, DZ, DY), f32), pltpu.VMEM((INNER, DZ, DY), f32),
                sem((4,)), sem((2,)), sem((2,)),
            ],
            flops=2 * INNER * DZ * DY * 5632, nbytes=12 << 20,
        )(field, halo, pit, phase, damage, w, weight, diffusivity, rate, sums)
        outs = call(
            functools.partial(outer_kernel, last), f"outer{substep}",
            (whole, extra) + (() if last else (slab, slab)),
            [HBM, VMEM, VMEM, VMEM, HBM, HBM, HBM, VMEM, SMEM, SMEM, SMEM, SMEM, HBM, VMEM],
            (HBM, VMEM) + (() if last else (VMEM, VMEM)),
            [
                pltpu.VMEM((18, DZ, DY), f32), pltpu.VMEM((18, DZ, DY), bf16), pltpu.VMEM((18, DZ, DY), bf16),
                pltpu.VMEM((6, DZ, DY), bf16),
                pltpu.VMEM((6, DZ, DY), jnp.int32), pltpu.VMEM((6, DZ, DY), jnp.int32),
                pltpu.VMEM((6, DZ, DY), jnp.int32), pltpu.VMEM((6, DZ, DY), f32),
                sem((2,)), sem((1,)), sem((2,)),
            ],
            {12: 0}, flops=2 * 6 * DZ * DY * 5632, nbytes=6 << 20,
        )(field, halo, from_low, from_high, pit, phase, damage, w, weight, diffusivity, rate, sums, out, more)
        if last:
            field, ends = outs
        else:
            field, pack, up, down = outs
    every = lax.all_gather(ends, "gz", axis=0)
    return call(
        functools.partial(depth_kernel, blocks), "depth", struct(DZ, DX, DY),
        [HBM, VMEM, SMEM], HBM,
        [pltpu.VMEM((DX, DZ, DY), f32), pltpu.VMEM((DZ, DX, DY), f32), sem((4,)), sem((4,))],
        nbytes=6 << 20,
    )(field, every, solve)


def solution(mesh):
    block = P("gz", "gx", "gy")
    in_specs = (block, block, block, P(), block, P(), P(), P())
    return jax.shard_map(local, mesh=mesh, in_specs=in_specs, out_specs=block, check_vma=False)
```

```python
import functools

import jax
import jax.numpy as jnp
import numpy as np
from jax import lax
from jax.experimental import pallas as pl
from jax.experimental.pallas import tpu as pltpu
from jax.sharding import PartitionSpec as P

DZ, DX, DY = 64, 32, 256
BONDS = 28
INNER = DX - 6
OUTER = [0, 1, 2, DX - 3, DX - 2, DX - 1]
f32, bf16 = jnp.float32, jnp.bfloat16
lateral_step = 0.02
dissolve_step = 0.25

VMEM = pl.BlockSpec(memory_space=pltpu.VMEM)
SMEM = pl.BlockSpec(memory_space=pltpu.SMEM)
HBM = pl.BlockSpec(memory_space=pltpu.HBM)
SEM = pltpu.SemaphoreType.DMA


def call(kernel, name, out_shape, in_specs, out_specs, scratch=(), flops=0, nbytes=1 << 20, limit=16):
    return pl.pallas_call(
        kernel,
        name=name,
        out_shape=out_shape,
        in_specs=in_specs,
        out_specs=out_specs,
        scratch_shapes=list(scratch),
        cost_estimate=pl.CostEstimate(flops=flops, bytes_accessed=nbytes, transcendentals=0),
        compiler_params=pltpu.CompilerParams(vmem_limit_bytes=limit << 20),
    )


def struct(*dims, dtype=f32):
    return jax.ShapeDtypeStruct(dims, dtype)


PARTS = tuple(struct(n, DZ, DY, dtype=t) for t in (f32, bf16, bf16) for n in (INNER, 6))
PACK = struct(2, DZ, 128)
SLABS = struct(7, DZ, 128)
WHOLE = struct(DX, DZ, DY)


def lanes():
    return lax.broadcasted_iota(jnp.int32, (DZ, 128), 1)


def add_to_pack(pack, row, x):
    slot = 8 * (x % 16)
    lane = lanes()
    last = pltpu.roll(row[:, 128:], (slot + 3) % 128, 1)
    first = pltpu.roll(row[:, :128], (slot + 4) % 128, 1)
    pack = jnp.where((lane >= slot) & (lane < slot + 3), last, pack)
    return jnp.where((lane >= slot + 4) & (lane < slot + 7), first, pack)


def split(value):
    high = value.astype(bf16)
    return high, (value - high.astype(f32)).astype(bf16)


def edge_window(before, after, x):
    slot = 8 * ((x + 13) % 16)
    lane = lanes()
    window = pltpu.roll(jnp.where(lane >= slot, before, after), (128 - slot) % 128, 1)
    high = window.astype(bf16).astype(f32)
    low = pltpu.roll(window - high, 64, 1)
    return jnp.concatenate([jnp.where(lane < 64, high, low).astype(bf16), high.astype(bf16)], axis=1)


def total_weight(weight):
    total = weight[0]
    for bond in range(1, BONDS):
        total = total + weight[bond]
    return total


def prepare_kernel(offsets, weight, diffusivity, rate, pit, phase, damage, w_ref, move, gain, table, pv, hv, dv, sem):
    def copies(group):
        return [
            pltpu.make_async_copy(source.at[:, x, :], target.at[x], sem.at[group])
            for x in range(8 * group, 8 * group + 8)
            for source, target in ((pit, pv), (phase, hv), (damage, dv))
        ]

    for group in range(4):
        for copy in copies(group):
            copy.start()
    for place in range(49):
        table[place] = jnp.float32(0.0)
    for bond in range(BONDS):
        place = (offsets[0, bond] + 3) * 7 + offsets[1, bond] + 3
        table[place] = table[place] + weight[bond]
    diff = lax.broadcasted_iota(jnp.int32, (DY, DY), 0) - lax.broadcasted_iota(jnp.int32, (DY, DY), 1) + 3

    @pl.loop(0, 7)
    def _(first):
        band = jnp.zeros((DY, DY), f32)
        for second in range(7):
            band = jnp.where(diff == second, table[first * 7 + second], band)
        w_ref[first], w_ref[7 + first] = split(band)

    lane = lax.broadcasted_iota(jnp.int32, (128, DY), 0)
    column = lax.broadcasted_iota(jnp.int32, (128, DY), 1)
    place = lane % 8
    which = jnp.where(place < 4, place - column, 255 + place - column)
    which = jnp.where((place == 3) | (place == 7), -1, which)
    which = jnp.where((which >= 0) & (which < 7), which, -100) + 7 * ((lane % 64) // 8)
    edge = jnp.zeros((128, DY), f32)
    for place in range(49):
        edge = jnp.where(which == place, table[place], edge)
    high, low = split(edge)
    w_ref[14, :128, :] = high
    w_ref[14, 128:, :] = jnp.where(lane < 64, low.astype(f32), 0.0).astype(bf16)

    def look(ids, values, scale):
        value = jnp.where(ids == 0, values[0] * scale, values[1] * scale)
        return jnp.where(ids < 2, value, jnp.where(ids == 2, values[2] * scale, values[3] * scale))

    for group in range(4):
        for copy in copies(group):
            copy.wait()

        @pl.loop(8 * group, 8 * group + 8)
        def _(x):
            ids = hv[x]
            move[x] = look(ids, diffusivity, lateral_step) * (1.0 + 0.5 * dv[x].astype(f32))
            gain[x] = look(ids, rate, dissolve_step) * pv[x].astype(f32)


def right_side(w_ref):
    bands = [w_ref[a] for a in range(7)]
    return jnp.concatenate(bands + bands + [w_ref[7 + a] for a in range(7)] + [w_ref[14]], axis=0)


def flat(value):
    return value.reshape(value.shape[0] * DZ, DY)


def stepped(center, flux, move, gain, weight_sum):
    return center + move * (flux - weight_sum * center) + gain * (1.0 - center)


def first_kernel(conc, mid, end, mid_high, end_high, mid_low, end_low, pack, up, down, buf, sem):
    for x in range(DX):
        pltpu.make_async_copy(conc.at[:, x, :], buf.at[x], sem.at[x // 8]).start()
    for group in range(4):
        for x in range(8 * group, 8 * group + 8):
            pltpu.make_async_copy(conc.at[:, x, :], buf.at[x], sem.at[group]).wait()
        if group % 2 == 0:
            packed = jnp.zeros((DZ, 128), f32)
        for x in range(8 * group, 8 * group + 8):
            row = buf[x]
            high, low = split(row)
            if x in OUTER:
                place = OUTER.index(x)
                end[place], end_high[place], end_low[place] = row, high, low
            else:
                mid[x - 3], mid_high[x - 3], mid_low[x - 3] = row, high, low
            packed = add_to_pack(packed, row, x)
        if group % 2:
            pack[group // 2] = packed
    fill_slabs(lambda row: buf[OUTER[row]], up, down)


def fill_slabs(row_of, up, down):
    for row in range(3):
        for half in range(2):
            part = slice(128 * half, 128 * half + 128)
            down[2 * row + half] = row_of(row)[:, part]
            up[2 * row + half] = row_of(3 + row)[:, part]
    down[6] = jnp.zeros((DZ, 128), f32)
    up[6] = jnp.zeros((DZ, 128), f32)


def join_kernel(left, right, up_in, down_in, halo, up, down):
    lane = lanes()
    for group in range(2):
        halo[group] = jnp.where(lane % 8 < 4, left[group], right[group])
    for slab in range(6):
        up[slab] = up_in[slab]
        down[slab] = down_in[slab]
    up[6] = halo[1]
    down[6] = halo[0]


CHUNK = INNER // 2


def row_range(mid, end, start, count):
    pieces = []
    stop = start + count
    if start < 3:
        pieces.append(end[start : min(stop, 3)])
    if stop > 3 and start < DX - 3:
        pieces.append(mid[max(start, 3) - 3 : min(stop, DX - 3) - 3])
    if stop > DX - 3:
        pieces.append(end[max(start, DX - 3) - DX + 6 : stop - DX + 6])
    pieces = [flat(piece) for piece in pieces]
    return pieces[0] if len(pieces) == 1 else jnp.concatenate(pieces, axis=0)


def inner_kernel(
    last, mid, mid_high, end_high, mid_low, end_low, halo, move, gain, w_ref, weight, sums,
    out, out_high, out_low, extra, edges,
):
    for x in range(3, DX - 3):
        group = (x + 13) // 16 - 1
        edges[x - 3] = edge_window(halo[group], halo[min(group + 1, 1)], x)
    weight_sum = total_weight(weight)
    packed = [jnp.zeros((DZ, 128), f32)] * 2
    for chunk in range(2):
        start = CHUNK * chunk
        highs = [row_range(mid_high, end_high, start + a, CHUNK) for a in range(7)]
        lows = [row_range(mid_low, end_low, start + a, CHUNK) for a in range(7)]
        left = highs + lows + highs + [flat(edges[start : start + CHUNK])]
        flux = jnp.dot(jnp.concatenate(left, axis=1), right_side(w_ref), preferred_element_type=f32)
        for i in range(CHUNK):
            row, x = start + i, start + i + 3
            new = stepped(mid[row], flux[DZ * i : DZ * i + DZ], move[x], gain[x], weight_sum)
            out[row] = new
            if not last:
                out_high[row], out_low[row] = split(new)
                packed[x // 16] = add_to_pack(packed[x // 16], new, x)
    if last:
        extra[...] = jnp.zeros_like(extra)
        depth_sums(out, sums, extra, 3, INNER, 0)
    else:
        for group in range(2):
            extra[group] = packed[group]


def depth_sums(rows, sums, extra, start, count, first):
    own = lax.axis_index("gz")
    below = jnp.zeros((count, DY), f32)
    above = jnp.zeros((count, DY), f32)
    for z in range(DZ):
        value = rows[first : first + count, z, :]
        below = below + sums[own, z] * value
        above = above + sums[own, DZ + z] * value
    extra[0, start : start + count, :] = below
    extra[1, start : start + count, :] = above


def outer_kernel(
    last, end, mid_high, end_high, mid_low, end_low, halo, from_low, from_high, move, gain, w_ref, weight, sums,
    extra_in, out, *rest,
):
    if last:
        (extra,) = rest
    else:
        out_high, out_low, extra, up, down = rest
    groups = [from_low[6], halo[0], halo[1], from_high[6]]
    edges = []
    for x in OUTER:
        group = (x + 13) // 16
        edges.append(edge_window(groups[group], groups[min(group + 1, 3)], x))

    def halo_rows(slabs):
        rows = [split(jnp.concatenate([slabs[2 * row], slabs[2 * row + 1]], axis=1)) for row in range(3)]
        return [row[0] for row in rows], [row[1] for row in rows]

    low_halo, high_halo = halo_rows(from_low), halo_rows(from_high)

    def taps(which, mid_part, end_part):
        top = low_halo[which] + [end_part[i] for i in range(3)] + [mid_part[i] for i in range(3)]
        bottom = [mid_part[INNER - 3 + i] for i in range(3)] + [end_part[3 + i] for i in range(3)]
        bottom = bottom + high_halo[which]
        return [jnp.concatenate(top[a : a + 3] + bottom[a : a + 3], axis=0) for a in range(7)]

    highs, lows = taps(0, mid_high, end_high), taps(1, mid_low, end_low)
    left = highs + lows + highs + [jnp.concatenate(edges, axis=0)]
    flux = jnp.dot(jnp.concatenate(left, axis=1), right_side(w_ref), preferred_element_type=f32)
    weight_sum = total_weight(weight)
    packed = [extra_in[0], extra_in[1]]
    for row, x in enumerate(OUTER):
        new = stepped(end[row], flux[DZ * row : DZ * row + DZ], move[x], gain[x], weight_sum)
        out[row] = new
        if not last:
            out_high[row], out_low[row] = split(new)
            packed[x // 16] = add_to_pack(packed[x // 16], new, x)
    if last:
        extra[...] = extra_in[...]
        depth_sums(out, sums, extra, 0, 3, 0)
        depth_sums(out, sums, extra, DX - 3, 3, 3)
    else:
        for group in range(2):
            extra[group] = packed[group]
        fill_slabs(lambda row: out[row], up, down)


def depth_tables(blocks):
    stiff = 3.0 * DZ * DZ
    count = DZ * blocks
    diagonal = np.full(count, 1.0 + 2.0 * stiff)
    diagonal[0] = diagonal[-1] = 1.0 + stiff
    fore = diagonal.copy()
    for i in range(1, count):
        fore[i] = diagonal[i] - stiff * stiff / fore[i - 1]
    back = diagonal.copy()
    for i in range(count - 2, -1, -1):
        back[i] = diagonal[i] - stiff * stiff / back[i + 1]
    sums = np.zeros((blocks, 2 * DZ))
    solve = np.zeros((blocks, 2 * DZ + 2 * blocks))
    for block in range(blocks):
        start, end = block * DZ, block * DZ + DZ - 1
        for z in range(DZ):
            sums[block, z] = np.prod(stiff / fore[start + z : end])
            sums[block, DZ + z] = np.prod(stiff / back[start + 1 : start + z + 1])
            solve[block, z] = stiff / fore[start + z - 1] if start + z else 0.0
            solve[block, DZ + z] = 1.0 / fore[start + z]
        if block < blocks - 1:
            solve[block, 2 * DZ - 1] = 1.0 / (fore[end] - stiff * stiff / back[end + 1])
        for other in range(blocks):
            if other < block:
                solve[block, 2 * DZ + other] = np.prod(stiff / fore[other * DZ + DZ - 1 : start])
            if other > block:
                solve[block, 2 * DZ + blocks + other] = np.prod(stiff / back[end + 1 : other * DZ + 1])
    return jnp.asarray(sums, f32), jnp.asarray(solve, f32)


def depth_kernel(blocks, mid, end, every, solve, out, buf, sweep, out_sem):
    for row, x in enumerate(OUTER):
        buf[:, x, :] = end[row]
    for row in range(INNER):
        buf[:, 3 + row, :] = mid[row]
    own = lax.axis_index("gz")
    stiff = 3.0 * DZ * DZ
    above = jnp.zeros((DX, DY), f32)
    below = jnp.zeros((DX, DY), f32)
    for block in range(blocks):
        above = above + solve[own, 2 * DZ + block] * every[block, 0]
        below = below + solve[own, 2 * DZ + blocks + block] * every[block, 1]
    value = above
    for z in range(DZ):
        carried = value if z == 0 else solve[own, z] * value
        value = buf[z] + carried
        sweep[z] = value
    value = (value + below) * solve[own, 2 * DZ - 1]
    for z in range(DZ - 1, -1, -1):
        if z < DZ - 1:
            value = (sweep[z] + stiff * value) * solve[own, DZ + z]
        sweep[z] = 2.0 * value - buf[z]
        if z % 16 == 0:
            part = pl.ds(z, 16)
            pltpu.make_async_copy(sweep.at[part], out.at[part], out_sem.at[z // 16]).start()
    for z in range(0, DZ, 16):
        part = pl.ds(z, 16)
        pltpu.make_async_copy(sweep.at[part], out.at[part], out_sem.at[z // 16]).wait()


def shift(value, axis, step):
    count = lax.axis_size(axis)
    return lax.ppermute(value, axis, [(i, (i + step) % count) for i in range(count)])


def local(conc, pit, phase, offsets, damage, weight, diffusivity, rate):
    blocks = lax.axis_size("gz")
    sums, solve = depth_tables(blocks)
    *parts, pack, up, down = call(
        first_kernel, "first", PARTS + (PACK, SLABS, SLABS), [HBM], (VMEM,) * 9,
        [pltpu.VMEM((DX, DZ, DY), f32), SEM((4,))], nbytes=4 << 20, limit=50,
    )(conc)
    w, move, gain = call(
        prepare_kernel, "prepare", (struct(15, DY, DY, dtype=bf16), WHOLE, WHOLE),
        [SMEM] * 4 + [HBM] * 3, (VMEM,) * 3,
        [pltpu.SMEM((64,), f32)] + [pltpu.VMEM((DX, DZ, DY), jnp.int32)] * 3 + [SEM((4,))],
        nbytes=8 << 20, limit=47,
    )(offsets.T, weight, diffusivity, rate, pit, phase, damage)
    for substep in range(2):
        last = substep == 1
        left, right = shift(pack, "gy", 1), shift(pack, "gy", -1)
        halo, up, down = call(
            join_kernel, "join", (PACK, SLABS, SLABS), [VMEM] * 4, (VMEM,) * 3,
        )(left, right, up, down)
        from_low, from_high = shift(up, "gx", 1), shift(down, "gx", -1)
        mid, end, mid_high, end_high, mid_low, end_low = parts
        extra = struct(2, DX, DY) if last else PACK
        tiny = struct(1, 16, 128, dtype=bf16)
        inner_split = (tiny, tiny) if last else (PARTS[2], PARTS[4])
        new_mid, new_mid_high, new_mid_low, more = call(
            functools.partial(inner_kernel, last), f"inner{substep}", (PARTS[0],) + inner_split + (extra,),
            [VMEM] * 9 + [SMEM] * 2, (VMEM,) * 4, [pltpu.VMEM((INNER, DZ, DY), bf16)],
            flops=2 * INNER * DZ * DY * 5632, nbytes=12 << 20,
        )(mid, mid_high, end_high, mid_low, end_low, halo, move, gain, w, weight, sums)
        outs = call(
            functools.partial(outer_kernel, last), f"outer{substep}",
            (PARTS[1],) + ((extra,) if last else (PARTS[3], PARTS[5], PACK, SLABS, SLABS)),
            [VMEM] * 11 + [SMEM] * 2 + [VMEM], (VMEM,) * (2 if last else 6),
            flops=2 * 6 * DZ * DY * 5632, nbytes=6 << 20,
        )(end, mid_high, end_high, mid_low, end_low, halo, from_low, from_high, move, gain, w, weight, sums, more)
        if last:
            new_end, ends = outs
        else:
            new_end, new_end_high, new_end_low, pack, up, down = outs
            parts = [new_mid, new_end, new_mid_high, new_end_high, new_mid_low, new_end_low]
    every = lax.all_gather(ends, "gz", axis=0)
    return call(
        functools.partial(depth_kernel, blocks), "depth", struct(DZ, DX, DY),
        [VMEM, VMEM, VMEM, SMEM], HBM,
        [pltpu.VMEM((DZ, DX, DY), f32), pltpu.VMEM((DZ, DX, DY), f32), SEM((4,))], nbytes=6 << 20,
    )(new_mid, new_end, every, solve)


def solution(mesh):
    block = P("gz", "gx", "gy")
    in_specs = (block, block, block, P(), block, P(), P(), P())
    return jax.shard_map(local, mesh=mesh, in_specs=in_specs, out_specs=block, check_vma=False)
```

```python
import functools

import jax
import jax.numpy as jnp
import numpy as np
from jax import lax
from jax.experimental import pallas as pl
from jax.experimental.pallas import tpu as pltpu
from jax.sharding import PartitionSpec as P

DZ, DX, DY = 64, 32, 256
BONDS = 28
INNER = DX - 6
OUTER = [0, 1, 2, DX - 3, DX - 2, DX - 1]
f32, bf16 = jnp.float32, jnp.bfloat16
lateral_step = 0.02
dissolve_step = 0.25

VMEM = pl.BlockSpec(memory_space=pltpu.VMEM)
SMEM = pl.BlockSpec(memory_space=pltpu.SMEM)
HBM = pl.BlockSpec(memory_space=pltpu.HBM)
SEM = pltpu.SemaphoreType.DMA


def call(kernel, name, out_shape, in_specs, out_specs, scratch=(), flops=0, nbytes=1 << 20, limit=16):
    return pl.pallas_call(
        kernel,
        name=name,
        out_shape=out_shape,
        in_specs=in_specs,
        out_specs=out_specs,
        scratch_shapes=list(scratch),
        cost_estimate=pl.CostEstimate(flops=flops, bytes_accessed=nbytes, transcendentals=0),
        compiler_params=pltpu.CompilerParams(vmem_limit_bytes=limit << 20),
    )


def struct(*dims, dtype=f32):
    return jax.ShapeDtypeStruct(dims, dtype)


PARTS = tuple(struct(n, DZ, DY, dtype=t) for t in (f32, bf16, bf16) for n in (INNER, 6))
PACK = struct(2, DZ, 128)
SLABS = struct(7, DZ, 128)
WHOLE = struct(DX, DZ, DY)


def lanes():
    return lax.broadcasted_iota(jnp.int32, (DZ, 128), 1)


def at_lanes(pack, row, source, target, count):
    lane = lanes()
    moved = pltpu.roll(row, (target - source) % 128, 1)
    return jnp.where((lane >= target) & (lane < target + count), moved, pack)


def two_sides(left, right):
    return jnp.where(lanes() % 8 < 4, left, right)


def split(value):
    high = value.astype(bf16)
    return high, (value - high.astype(f32)).astype(bf16)


def edge_window(before, after, x):
    slot = 8 * ((x + 13) % 16)
    lane = lanes()
    window = pltpu.roll(jnp.where(lane >= slot, before, after), (128 - slot) % 128, 1)
    high = window.astype(bf16).astype(f32)
    low = pltpu.roll(window - high, 64, 1)
    return jnp.concatenate([jnp.where(lane < 64, high, low).astype(bf16), high.astype(bf16)], axis=1)


def total_weight(weight):
    total = weight[0]
    for bond in range(1, BONDS):
        total = total + weight[bond]
    return total


def prepare_kernel(offsets, weight, diffusivity, rate, pit, phase, damage, w_ref, move, gain, table, to_high, to_low, pv, hv, dv, sem):
    def copies(group):
        return [
            pltpu.make_async_copy(source.at[:, x, :], target.at[x], sem.at[group])
            for x in range(8 * group, 8 * group + 8)
            for source, target in ((pit, pv), (phase, hv), (damage, dv))
        ]

    for group in range(4):
        for copy in copies(group):
            copy.start()
    for place in range(49):
        table[place] = jnp.float32(0.0)
    for bond in range(BONDS):
        place = (offsets[0, bond] + 3) * 7 + offsets[1, bond] + 3
        table[place] = table[place] + weight[bond]
    diff = lax.broadcasted_iota(jnp.int32, (DY, DY), 0) - lax.broadcasted_iota(jnp.int32, (DY, DY), 1) + 3

    @pl.loop(0, 7)
    def _(first):
        band = jnp.zeros((DY, DY), f32)
        for second in range(7):
            band = jnp.where(diff == second, table[first * 7 + second], band)
        w_ref[first], w_ref[7 + first] = split(band)

    lane = lax.broadcasted_iota(jnp.int32, (128, DY), 0)
    column = lax.broadcasted_iota(jnp.int32, (128, DY), 1)
    place = lane % 8
    which = jnp.where(place < 4, place - column, 255 + place - column)
    which = jnp.where((place == 3) | (place == 7), -1, which)
    which = jnp.where((which >= 0) & (which < 7), which, -100) + 7 * ((lane % 64) // 8)
    edge = jnp.zeros((128, DY), f32)
    for place in range(49):
        edge = jnp.where(which == place, table[place], edge)
    high, low = split(edge)
    w_ref[14, :128, :] = high
    w_ref[14, 128:, :] = jnp.where(lane < 64, low.astype(f32), 0.0).astype(bf16)

    def look(ids, values, scale):
        value = jnp.where(ids == 0, values[0] * scale, values[1] * scale)
        return jnp.where(ids < 2, value, jnp.where(ids == 2, values[2] * scale, values[3] * scale))

    for group in range(4):
        for copy in copies(group):
            copy.wait()

        @pl.loop(8 * group, 8 * group + 8)
        def _(x):
            ids = hv[x]
            move[x] = look(ids, diffusivity, lateral_step) * (1.0 + 0.5 * dv[x].astype(f32))
            gain[x] = look(ids, rate, dissolve_step) * pv[x].astype(f32)

        if group % 2 == 0:
            high, low = jnp.zeros((DZ, 128), f32), jnp.zeros((DZ, 128), f32)
        for x in range(8 * group, 8 * group + 8):
            slot = 8 * (x % 16)
            high = at_lanes(high, move[x, :, 128:], 125, slot, 3)
            high = at_lanes(high, gain[x, :, 128:], 125, slot + 4, 3)
            low = at_lanes(low, gain[x, :, :128], 0, slot, 3)
            low = at_lanes(low, move[x, :, :128], 0, slot + 4, 3)
        if group % 2:
            to_high[group // 2], to_low[group // 2] = high, low


def right_side(w_ref):
    bands = [w_ref[a] for a in range(7)]
    return jnp.concatenate(bands + bands + [w_ref[7 + a] for a in range(7)] + [w_ref[14]], axis=0)


def flat(value):
    return value.reshape(value.shape[0] * DZ, DY)


def stepped(center, flux, move, gain, weight_sum):
    return center + move * (flux - weight_sum * center) + gain * (1.0 - center)


def first_kernel(conc, mid, end, mid_high, end_high, mid_low, end_low, lasts, firsts, up, down, buf, sem):
    for x in range(DX):
        pltpu.make_async_copy(conc.at[:, x, :], buf.at[x], sem.at[x // 8]).start()
    for group in range(4):
        for x in range(8 * group, 8 * group + 8):
            pltpu.make_async_copy(conc.at[:, x, :], buf.at[x], sem.at[group]).wait()
        if group % 2 == 0:
            high_side, low_side = jnp.zeros((DZ, 128), f32), jnp.zeros((DZ, 128), f32)
        for x in range(8 * group, 8 * group + 8):
            row = buf[x]
            high, low = split(row)
            if x in OUTER:
                place = OUTER.index(x)
                end[place], end_high[place], end_low[place] = row, high, low
            else:
                mid[x - 3], mid_high[x - 3], mid_low[x - 3] = row, high, low
            slot = 8 * (x % 16)
            high_side = at_lanes(high_side, row[:, 128:], 122, slot, 6)
            low_side = at_lanes(low_side, row[:, :128], 0, slot, 6)
        if group % 2:
            lasts[group // 2], firsts[group // 2] = high_side, low_side
    fill_slabs(lambda row: buf[OUTER[row]], up, down)
    down[6] = jnp.zeros((DZ, 128), f32)
    up[6] = jnp.zeros((DZ, 128), f32)


def fill_slabs(row_of, up, down):
    for row in range(3):
        for half in range(2):
            part = slice(128 * half, 128 * half + 128)
            down[2 * row + half] = row_of(row)[:, part]
            up[2 * row + half] = row_of(3 + row)[:, part]


def join_kernel(left, right, lasts, firsts, up_in, down_in, strips, up, down):
    for group in range(2):
        strips[0, group] = two_sides(left[group], pltpu.roll(lasts[group], 1, 1))
        strips[1, group] = two_sides(pltpu.roll(left[group], 125, 1), pltpu.roll(right[group], 4, 1))
        strips[2, group] = two_sides(firsts[group], pltpu.roll(right[group], 1, 1))
    for slab in range(6):
        up[slab] = up_in[slab]
        down[slab] = down_in[slab]
    lane = lanes()
    up[6] = jnp.where(
        lane >= 104, strips[1, 1],
        jnp.where(lane >= 72, pltpu.roll(strips[0, 1], 96, 1), pltpu.roll(strips[2, 1], 64, 1)),
    )
    down[6] = jnp.where(
        lane < 32, strips[1, 0],
        jnp.where(lane < 64, pltpu.roll(strips[0, 0], 32, 1), pltpu.roll(strips[2, 0], 64, 1)),
    )


def strip_taps(table, first, second, third):
    place = lanes() % 4

    def moved(value, step):
        return pltpu.roll(value, step % 128, 1)

    columns = [
        first,
        jnp.where(place < 2, moved(first, -1), moved(second, 2)),
        jnp.where(place < 1, moved(first, -2), moved(second, 1)),
        second,
        jnp.where(place < 2, moved(second, -1), moved(third, 2)),
        jnp.where(place < 1, moved(second, -2), moved(third, 1)),
        third,
    ]
    sums = []
    for a in range(7):
        total = table[7 * a] * columns[0]
        for second_index in range(1, 7):
            total = total + table[7 * a + second_index] * columns[second_index]
        sums.append(total)
    return sums


def strip_flux(taps, group):
    lane = lanes()
    total = jnp.zeros((DZ, 128), f32)
    zero = jnp.zeros((DZ, 128), f32)
    for a in range(7):
        step = 8 * (a - 3)
        own, after, before = (
            zero if taps[g] is None else taps[g][a] for g in (group, (group + 1) % 3, (group + 2) % 3)
        )
        if step == 0:
            total = total + own
        elif step > 0:
            total = total + pltpu.roll(jnp.where(lane >= step, own, after), 128 - step, 1)
        else:
            total = total + pltpu.roll(jnp.where(lane < 128 + step, own, before), -step, 1)
    return total


CHUNK = INNER // 2


def row_range(mid, end, start, count):
    pieces = []
    stop = start + count
    if start < 3:
        pieces.append(end[start : min(stop, 3)])
    if stop > 3 and start < DX - 3:
        pieces.append(mid[max(start, 3) - 3 : min(stop, DX - 3) - 3])
    if stop > DX - 3:
        pieces.append(end[max(start, DX - 3) - DX + 6 : stop - DX + 6])
    pieces = [flat(piece) for piece in pieces]
    return pieces[0] if len(pieces) == 1 else jnp.concatenate(pieces, axis=0)


def inner_kernel(
    last, mid, mid_high, end_high, mid_low, end_low, strips, move, gain, w_ref, weight, sums, table,
    out, out_high, out_low, extra, edges,
):
    halo = strips.at[0 if last else 1]
    for x in range(3, DX - 3):
        group = (x + 13) // 16 - 1
        edges[x - 3] = edge_window(halo[group], halo[min(group + 1, 1)], x)
    weight_sum = total_weight(weight)
    for chunk in range(2):
        start = CHUNK * chunk
        highs = [row_range(mid_high, end_high, start + a, CHUNK) for a in range(7)]
        lows = [row_range(mid_low, end_low, start + a, CHUNK) for a in range(7)]
        left = highs + lows + highs + [flat(edges[start : start + CHUNK])]
        flux = jnp.dot(jnp.concatenate(left, axis=1), right_side(w_ref), preferred_element_type=f32)
        for i in range(CHUNK):
            row, x = start + i, start + i + 3
            new = stepped(mid[row], flux[DZ * i : DZ * i + DZ], move[x], gain[x], weight_sum)
            out[row] = new
            if not last:
                out_high[row], out_low[row] = split(new)
    if last:
        extra[...] = jnp.zeros_like(extra)
        depth_sums(out, sums, extra, 3, INNER, 0)
    else:
        taps = [strip_taps(table, strips[0, g], strips[1, g], strips[2, g]) for g in range(2)] + [None]
        for group in range(2):
            extra[group] = strip_flux(taps, group)


def depth_sums(rows, sums, extra, start, count, first):
    own = lax.axis_index("gz")
    below = jnp.zeros((count, DY), f32)
    above = jnp.zeros((count, DY), f32)
    for z in range(DZ):
        value = rows[first : first + count, z, :]
        below = below + sums[own, z] * value
        above = above + sums[own, DZ + z] * value
    extra[0, start : start + count, :] = below
    extra[1, start : start + count, :] = above


def outer_kernel(
    last, end, mid_high, end_high, mid_low, end_low, strips, from_low, from_high, move, gain, w_ref, weight, sums,
    extra_in, *rest,
):
    if last:
        out, extra = rest
    else:
        table, coefs_left, coefs_right, out, out_high, out_low, extra, up, down = rest
    halo = strips.at[0 if last else 1]
    groups = [from_low[6], halo[0], halo[1], from_high[6]]
    edges = []
    for x in OUTER:
        group = (x + 13) // 16
        edges.append(edge_window(groups[group], groups[min(group + 1, 3)], x))

    def halo_rows(slabs):
        rows = [split(jnp.concatenate([slabs[2 * row], slabs[2 * row + 1]], axis=1)) for row in range(3)]
        return [row[0] for row in rows], [row[1] for row in rows]

    low_halo, high_halo = halo_rows(from_low), halo_rows(from_high)

    def taps(which, mid_part, end_part):
        top = low_halo[which] + [end_part[i] for i in range(3)] + [mid_part[i] for i in range(3)]
        bottom = [mid_part[INNER - 3 + i] for i in range(3)] + [end_part[3 + i] for i in range(3)]
        bottom = bottom + high_halo[which]
        return [jnp.concatenate(top[a : a + 3] + bottom[a : a + 3], axis=0) for a in range(7)]

    highs, lows = taps(0, mid_high, end_high), taps(1, mid_low, end_low)
    left = highs + lows + highs + [jnp.concatenate(edges, axis=0)]
    flux = jnp.dot(jnp.concatenate(left, axis=1), right_side(w_ref), preferred_element_type=f32)
    weight_sum = total_weight(weight)
    for row, x in enumerate(OUTER):
        new = stepped(end[row], flux[DZ * row : DZ * row + DZ], move[x], gain[x], weight_sum)
        out[row] = new
        if not last:
            out_high[row], out_low[row] = split(new)
    if last:
        extra[...] = extra_in[...]
        depth_sums(out, sums, extra, 0, 3, 0)
        depth_sums(out, sums, extra, DX - 3, 3, 3)
    else:
        fill_slabs(lambda row: out[row], up, down)
        lane = lanes()
        low, high = from_low[6], from_high[6]
        beyond = [
            jnp.where(lane < 64, pltpu.roll(high, 96, 1), pltpu.roll(low, 32, 1)),
            jnp.where(lane < 64, high, low),
            jnp.where(lane < 64, pltpu.roll(high, 64, 1), pltpu.roll(low, 64, 1)),
        ]
        taps = [None, None, strip_taps(table, *beyond)]
        for group in range(2):
            flux = extra_in[group] + strip_flux(taps, group)
            left, right = coefs_left[group], coefs_right[group]
            extra[0, group] = stepped(
                halo[group], flux, two_sides(left, right),
                two_sides(pltpu.roll(left, 124, 1), pltpu.roll(right, 4, 1)), weight_sum,
            )
        up[6] = extra[0, 1]
        down[6] = extra[0, 0]


def depth_tables(blocks):
    stiff = 3.0 * DZ * DZ
    count = DZ * blocks
    diagonal = np.full(count, 1.0 + 2.0 * stiff)
    diagonal[0] = diagonal[-1] = 1.0 + stiff
    fore = diagonal.copy()
    for i in range(1, count):
        fore[i] = diagonal[i] - stiff * stiff / fore[i - 1]
    back = diagonal.copy()
    for i in range(count - 2, -1, -1):
        back[i] = diagonal[i] - stiff * stiff / back[i + 1]
    sums = np.zeros((blocks, 2 * DZ))
    solve = np.zeros((blocks, 2 * DZ + 2 * blocks))
    for block in range(blocks):
        start, end = block * DZ, block * DZ + DZ - 1
        for z in range(DZ):
            sums[block, z] = np.prod(stiff / fore[start + z : end])
            sums[block, DZ + z] = np.prod(stiff / back[start + 1 : start + z + 1])
            solve[block, z] = stiff / fore[start + z - 1] if start + z else 0.0
            solve[block, DZ + z] = 1.0 / fore[start + z]
        if block < blocks - 1:
            solve[block, 2 * DZ - 1] = 1.0 / (fore[end] - stiff * stiff / back[end + 1])
        for other in range(blocks):
            if other < block:
                solve[block, 2 * DZ + other] = np.prod(stiff / fore[other * DZ + DZ - 1 : start])
            if other > block:
                solve[block, 2 * DZ + blocks + other] = np.prod(stiff / back[end + 1 : other * DZ + 1])
    return jnp.asarray(sums, f32), jnp.asarray(solve, f32)


def depth_kernel(blocks, mid, end, every, solve, out, buf, sweep, out_sem):
    for row, x in enumerate(OUTER):
        buf[:, x, :] = end[row]
    for row in range(INNER):
        buf[:, 3 + row, :] = mid[row]
    own = lax.axis_index("gz")
    stiff = 3.0 * DZ * DZ
    above = jnp.zeros((DX, DY), f32)
    below = jnp.zeros((DX, DY), f32)
    for block in range(blocks):
        above = above + solve[own, 2 * DZ + block] * every[block, 0]
        below = below + solve[own, 2 * DZ + blocks + block] * every[block, 1]
    value = above
    for z in range(DZ):
        carried = value if z == 0 else solve[own, z] * value
        value = buf[z] + carried
        sweep[z] = value
    value = (value + below) * solve[own, 2 * DZ - 1]
    for z in range(DZ - 1, -1, -1):
        if z < DZ - 1:
            value = (sweep[z] + stiff * value) * solve[own, DZ + z]
        sweep[z] = 2.0 * value - buf[z]
        if z % 16 == 0:
            part = pl.ds(z, 16)
            pltpu.make_async_copy(sweep.at[part], out.at[part], out_sem.at[z // 16]).start()
    for z in range(0, DZ, 16):
        part = pl.ds(z, 16)
        pltpu.make_async_copy(sweep.at[part], out.at[part], out_sem.at[z // 16]).wait()


def shift(value, axis, step):
    count = lax.axis_size(axis)
    return lax.ppermute(value, axis, [(i, (i + step) % count) for i in range(count)])


def local(conc, pit, phase, offsets, damage, weight, diffusivity, rate):
    blocks = lax.axis_size("gz")
    sums, solve = depth_tables(blocks)
    *parts, lasts, firsts, up, down = call(
        first_kernel, "first", PARTS + (PACK, PACK, SLABS, SLABS), [HBM], (VMEM,) * 10,
        [pltpu.VMEM((DX, DZ, DY), f32), SEM((4,))], nbytes=4 << 20, limit=50,
    )(conc)
    left, right = shift(lasts, "gy", 1), shift(firsts, "gy", -1)
    w, move, gain, table, to_high, to_low = call(
        prepare_kernel, "prepare", (struct(15, DY, DY, dtype=bf16), WHOLE, WHOLE, struct(64), PACK, PACK),
        [SMEM] * 4 + [HBM] * 3, (VMEM, VMEM, VMEM, SMEM, VMEM, VMEM),
        [pltpu.VMEM((DX, DZ, DY), jnp.int32)] * 3 + [SEM((4,))],
        nbytes=8 << 20, limit=47,
    )(offsets.T, weight, diffusivity, rate, pit, phase, damage)
    strips, up, down = call(
        join_kernel, "join", (struct(3, 2, DZ, 128), SLABS, SLABS), [VMEM] * 6, (VMEM,) * 3,
    )(left, right, lasts, firsts, up, down)
    for substep in range(2):
        last = substep == 1
        from_low, from_high = shift(up, "gx", 1), shift(down, "gx", -1)
        if not last:
            to_high, to_low, up, down = lax.optimization_barrier((to_high, to_low, up, down))
            coefs = [shift(to_high, "gy", 1), shift(to_low, "gy", -1)]
        mid, end, mid_high, end_high, mid_low, end_low = parts
        tiny = struct(1, 16, 128, dtype=bf16)
        inner_split = (tiny, tiny) if last else (PARTS[2], PARTS[4])
        new_mid, new_mid_high, new_mid_low, more = call(
            functools.partial(inner_kernel, last), f"inner{substep}",
            (PARTS[0],) + inner_split + ((struct(2, DX, DY) if last else PACK),),
            [VMEM] * 9 + [SMEM] * 3, (VMEM,) * 4, [pltpu.VMEM((INNER, DZ, DY), bf16)],
            flops=2 * INNER * DZ * DY * 5632, nbytes=12 << 20,
        )(mid, mid_high, end_high, mid_low, end_low, strips, move, gain, w, weight, sums, table)
        args = (end, mid_high, end_high, mid_low, end_low, strips, from_low, from_high, move, gain, w, weight, sums, more)
        specs = [VMEM] * 11 + [SMEM] * 2 + [VMEM]
        cost = dict(flops=2 * 6 * DZ * DY * 5632, nbytes=6 << 20)
        if last:
            new_end, ends = call(
                functools.partial(outer_kernel, last), "outer1", (PARTS[1], struct(2, DX, DY)), specs, (VMEM,) * 2, **cost
            )(*args)
        else:
            new_end, new_end_high, new_end_low, strips, up, down = call(
                functools.partial(outer_kernel, last), "outer0",
                (PARTS[1], PARTS[3], PARTS[5], struct(1, 2, DZ, 128), SLABS, SLABS),
                specs + [SMEM, VMEM, VMEM], (VMEM,) * 6, **cost,
            )(*args, table, *coefs)
            parts = [new_mid, new_end, new_mid_high, new_end_high, new_mid_low, new_end_low]
    every = lax.all_gather(ends, "gz", axis=0)
    return call(
        functools.partial(depth_kernel, blocks), "depth", struct(DZ, DX, DY),
        [VMEM, VMEM, VMEM, SMEM], HBM,
        [pltpu.VMEM((DZ, DX, DY), f32), pltpu.VMEM((DZ, DX, DY), f32), SEM((4,))], nbytes=6 << 20,
    )(new_mid, new_end, every, solve)


def solution(mesh):
    block = P("gz", "gx", "gy")
    in_specs = (block, block, block, P(), block, P(), P(), P())
    return jax.shard_map(local, mesh=mesh, in_specs=in_specs, out_specs=block, check_vma=False)
```

```python
import functools

import jax
import jax.numpy as jnp
import numpy as np
from jax import lax
from jax.experimental import pallas as pl
from jax.experimental.pallas import tpu as pltpu
from jax.sharding import PartitionSpec as P

DZ, DX, DY = 64, 32, 256
BONDS = 28
INNER = DX - 6
OUTER = [0, 1, 2, DX - 3, DX - 2, DX - 1]
f32, bf16 = jnp.float32, jnp.bfloat16
lateral_step = 0.02
dissolve_step = 0.25

VMEM = pl.BlockSpec(memory_space=pltpu.VMEM)
SMEM = pl.BlockSpec(memory_space=pltpu.SMEM)
HBM = pl.BlockSpec(memory_space=pltpu.HBM)
SEM = pltpu.SemaphoreType.DMA


def call(kernel, name, out_shape, in_specs, out_specs, scratch=(), flops=0, nbytes=1 << 20, limit=16):
    return pl.pallas_call(
        kernel,
        name=name,
        out_shape=out_shape,
        in_specs=in_specs,
        out_specs=out_specs,
        scratch_shapes=list(scratch),
        cost_estimate=pl.CostEstimate(flops=flops, bytes_accessed=nbytes, transcendentals=0),
        compiler_params=pltpu.CompilerParams(vmem_limit_bytes=limit << 20),
    )


def struct(*dims, dtype=f32):
    return jax.ShapeDtypeStruct(dims, dtype)


PARTS = tuple(struct(n, DZ, DY, dtype=t) for t in (f32, bf16, bf16) for n in (INNER, 6))
PACK = struct(2, DZ, 128)
SLABS = struct(7, DZ, 128)
WHOLE = struct(DX, DZ, DY)


def lanes():
    return lax.broadcasted_iota(jnp.int32, (DZ, 128), 1)


def at_lanes(pack, row, source, target, count):
    lane = lanes()
    moved = pltpu.roll(row, (target - source) % 128, 1)
    return jnp.where((lane >= target) & (lane < target + count), moved, pack)


def two_sides(left, right):
    return jnp.where(lanes() % 8 < 4, left, right)


def split(value):
    high = value.astype(bf16)
    return high, (value - high.astype(f32)).astype(bf16)


def add_middle(pack, row, x):
    slot = 8 * (x % 16)
    pack = at_lanes(pack, row[:, :128], 125, slot, 3)
    return at_lanes(pack, row[:, 128:], 0, slot + 4, 3)


def edge_window(before, after, x):
    slot = 8 * ((x + 13) % 16)
    lane = lanes()
    window = pltpu.roll(jnp.where(lane >= slot, before, after), (128 - slot) % 128, 1)
    high = window.astype(bf16).astype(f32)
    low = pltpu.roll(window - high, 64, 1)
    return jnp.concatenate([jnp.where(lane < 64, high, low).astype(bf16), high.astype(bf16)], axis=1)


def total_weight(weight):
    total = weight[0]
    for bond in range(1, BONDS):
        total = total + weight[bond]
    return total


def prepare_kernel(offsets, weight, diffusivity, rate, pit, phase, damage, mid, end, w_ref, move, gain, table, to_high, to_low, middle, pv, hv, dv, sem):
    def copies(group):
        return [
            pltpu.make_async_copy(source.at[:, x, :], target.at[x], sem.at[group])
            for x in range(8 * group, 8 * group + 8)
            for source, target in ((pit, pv), (phase, hv), (damage, dv))
        ]

    for group in range(4):
        for copy in copies(group):
            copy.start()
    for place in range(49):
        table[place] = jnp.float32(0.0)
    for bond in range(BONDS):
        place = (offsets[0, bond] + 3) * 7 + offsets[1, bond] + 3
        table[place] = table[place] + weight[bond]
    diff = lax.broadcasted_iota(jnp.int32, (128, 128), 0) - lax.broadcasted_iota(jnp.int32, (128, 128), 1) + 3
    blank = jnp.zeros((128, 128), bf16)
    for start in (0, 4):
        w_ref[start, :128, 128:] = blank
        w_ref[start + 3, 128:, :128] = blank
    for first in range(7):
        band = jnp.zeros((128, 128), f32)
        for second in range(7):
            band = jnp.where(diff == second, table[first * 7 + second], band)
        high, low = split(band)
        for out_row in range(2):
            row = first + out_row
            place = (slice(128 * (row % 2), 128 * (row % 2) + 128), slice(128 * out_row, 128 * out_row + 128))
            w_ref[(row // 2,) + place] = high
            w_ref[(4 + row // 2,) + place] = low
    lane = lax.broadcasted_iota(jnp.int32, (64, DY), 0)
    column = lax.broadcasted_iota(jnp.int32, (64, DY), 1)
    place = lane % 8
    first = lane // 8 - column // 128
    second = jnp.where(place < 4, place, 127 + place) - column % 128
    good = (place != 3) & (place != 7) & (first >= 0) & (first < 7) & (second >= 0) & (second < 7)
    which = jnp.where(good, 7 * first + second, -1)
    edge = jnp.zeros((64, DY), f32)
    for place in range(49):
        edge = jnp.where(which == place, table[place], edge)
    high, low = split(edge)
    for row, value in enumerate((high, high, low, jnp.zeros((64, DY), bf16))):
        w_ref[8, 64 * row : 64 * row + 64, :] = value
    packed = [jnp.zeros((DZ, 128), f32)] * 2
    for x in range(DX):
        packed[x // 16] = add_middle(packed[x // 16], end[OUTER.index(x)] if x in OUTER else mid[x - 3], x)
    middle[0], middle[1] = packed

    def look(ids, values, scale):
        value = jnp.where(ids == 0, values[0] * scale, values[1] * scale)
        return jnp.where(ids < 2, value, jnp.where(ids == 2, values[2] * scale, values[3] * scale))

    for group in range(4):
        for copy in copies(group):
            copy.wait()

        @pl.loop(8 * group, 8 * group + 8)
        def _(x):
            ids = hv[x]
            move[x] = look(ids, diffusivity, lateral_step) * (1.0 + 0.5 * dv[x].astype(f32))
            gain[x] = look(ids, rate, dissolve_step) * pv[x].astype(f32)

        if group % 2 == 0:
            high, low = jnp.zeros((DZ, 128), f32), jnp.zeros((DZ, 128), f32)
        for x in range(8 * group, 8 * group + 8):
            slot = 8 * (x % 16)
            high = at_lanes(high, move[x, :, 128:], 125, slot, 3)
            high = at_lanes(high, gain[x, :, 128:], 125, slot + 4, 3)
            low = at_lanes(low, gain[x, :, :128], 0, slot, 3)
            low = at_lanes(low, move[x, :, :128], 0, slot + 4, 3)
        if group % 2:
            to_high[group // 2], to_low[group // 2] = high, low


def right_side(w_ref):
    high, low = [w_ref[t] for t in range(4)], [w_ref[4 + t] for t in range(4)]
    return jnp.concatenate(high + high + low + [w_ref[8]], axis=0)


def pair_flux(pairs, high_of, low_of, edges, half, w_ref):
    part = slice(128 * half, 128 * half + 128)

    def side(row_of):
        return [jnp.concatenate([row_of(x - 3 + i)[:, part] for x in pairs], axis=0) for i in range(8)]

    high, low = side(high_of), side(low_of)
    left = jnp.concatenate(high + low + high + [edges], axis=1)
    flux = jnp.dot(left, right_side(w_ref), preferred_element_type=f32)

    def of(place, out_row):
        return flux[DZ * place : DZ * place + DZ, 128 * out_row : 128 * out_row + 128]

    return of


def stepped(center, flux, move, gain, weight_sum):
    return center + move * (flux - weight_sum * center) + gain * (1.0 - center)


def first_kernel(conc, mid, end, mid_high, end_high, mid_low, end_low, lasts, firsts, up, down, buf, sem):
    for x in range(DX):
        pltpu.make_async_copy(conc.at[:, x, :], buf.at[x], sem.at[x // 8]).start()
    for group in range(4):
        for x in range(8 * group, 8 * group + 8):
            pltpu.make_async_copy(conc.at[:, x, :], buf.at[x], sem.at[group]).wait()
        if group % 2 == 0:
            high_side, low_side = jnp.zeros((DZ, 128), f32), jnp.zeros((DZ, 128), f32)
        for x in range(8 * group, 8 * group + 8):
            row = buf[x]
            high, low = split(row)
            if x in OUTER:
                place = OUTER.index(x)
                end[place], end_high[place], end_low[place] = row, high, low
            else:
                mid[x - 3], mid_high[x - 3], mid_low[x - 3] = row, high, low
            slot = 8 * (x % 16)
            high_side = at_lanes(high_side, row[:, 128:], 122, slot, 6)
            low_side = at_lanes(low_side, row[:, :128], 0, slot, 6)
        if group % 2:
            lasts[group // 2], firsts[group // 2] = high_side, low_side
    fill_slabs(lambda row: buf[OUTER[row]], up, down)
    down[6] = jnp.zeros((DZ, 128), f32)
    up[6] = jnp.zeros((DZ, 128), f32)


def fill_slabs(row_of, up, down):
    for row in range(3):
        for half in range(2):
            part = slice(128 * half, 128 * half + 128)
            down[2 * row + half] = row_of(row)[:, part]
            up[2 * row + half] = row_of(3 + row)[:, part]


def join_kernel(left, right, lasts, firsts, up_in, down_in, strips, up, down):
    for group in range(2):
        strips[0, group] = two_sides(left[group], pltpu.roll(lasts[group], 1, 1))
        strips[1, group] = two_sides(pltpu.roll(left[group], 125, 1), pltpu.roll(right[group], 4, 1))
        strips[2, group] = two_sides(firsts[group], pltpu.roll(right[group], 1, 1))
    for slab in range(6):
        up[slab] = up_in[slab]
        down[slab] = down_in[slab]
    lane = lanes()
    up[6] = jnp.where(
        lane >= 104, strips[1, 1],
        jnp.where(lane >= 72, pltpu.roll(strips[0, 1], 96, 1), pltpu.roll(strips[2, 1], 64, 1)),
    )
    down[6] = jnp.where(
        lane < 32, strips[1, 0],
        jnp.where(lane < 64, pltpu.roll(strips[0, 0], 32, 1), pltpu.roll(strips[2, 0], 64, 1)),
    )


def strip_taps(table, first, second, third):
    place = lanes() % 4

    def moved(value, step):
        return pltpu.roll(value, step % 128, 1)

    columns = [
        first,
        jnp.where(place < 2, moved(first, -1), moved(second, 2)),
        jnp.where(place < 1, moved(first, -2), moved(second, 1)),
        second,
        jnp.where(place < 2, moved(second, -1), moved(third, 2)),
        jnp.where(place < 1, moved(second, -2), moved(third, 1)),
        third,
    ]
    sums = []
    for a in range(7):
        total = table[7 * a] * columns[0]
        for second_index in range(1, 7):
            total = total + table[7 * a + second_index] * columns[second_index]
        sums.append(total)
    return sums


def strip_flux(taps, group):
    lane = lanes()
    total = jnp.zeros((DZ, 128), f32)
    zero = jnp.zeros((DZ, 128), f32)
    for a in range(7):
        step = 8 * (a - 3)
        own, after, before = (
            zero if taps[g] is None else taps[g][a] for g in (group, (group + 1) % 3, (group + 2) % 3)
        )
        if step == 0:
            total = total + own
        elif step > 0:
            total = total + pltpu.roll(jnp.where(lane >= step, own, after), 128 - step, 1)
        else:
            total = total + pltpu.roll(jnp.where(lane < 128 + step, own, before), -step, 1)
    return total


def inner_kernel(
    last, mid, mid_high, end_high, mid_low, end_low, strips, middle, move, gain, w_ref, weight, sums, table,
    out, out_high, out_low, extra, new_middle,
):
    halo = strips.at[0 if last else 1]
    weight_sum = total_weight(weight)
    pairs = range(3, DX - 3, 2)

    def row_of(mid_part, end_part):
        return lambda x: end_part[OUTER.index(x)] if x in OUTER else mid_part[x - 3]

    packed = [jnp.zeros((DZ, 128), f32)] * 2
    for half in range(2):
        around = [
            two_sides(halo[g], middle[g]) if half == 0 else two_sides(middle[g], halo[g]) for g in range(2)
        ]
        edges = []
        for x in pairs:
            group = (x + 13) // 16 - 1
            edges.append(edge_window(around[group], around[min(group + 1, 1)], x))
        flux = pair_flux(
            pairs, row_of(mid_high, end_high), row_of(mid_low, end_low), jnp.concatenate(edges, axis=0), half, w_ref
        )
        part = slice(128 * half, 128 * half + 128)
        for place, first in enumerate(pairs):
            for out_row in range(2):
                x = first + out_row
                row = x - 3
                new = stepped(mid[row, :, part], flux(place, out_row), move[x, :, part], gain[x, :, part], weight_sum)
                out[row, :, part] = new
                if not last:
                    out_high[row, :, part], out_low[row, :, part] = split(new)
                    slot = 8 * (x % 16)
                    source, target = (125, slot) if half == 0 else (0, slot + 4)
                    packed[x // 16] = at_lanes(packed[x // 16], new, source, target, 3)
    if last:
        extra[...] = jnp.zeros_like(extra)
        depth_sums(out, sums, extra, 3, INNER, 0)
    else:
        new_middle[0], new_middle[1] = packed
        taps = [strip_taps(table, strips[0, g], strips[1, g], strips[2, g]) for g in range(2)] + [None]
        for group in range(2):
            extra[group] = strip_flux(taps, group)


def depth_sums(rows, sums, extra, start, count, first):
    own = lax.axis_index("gz")
    below = jnp.zeros((count, DY), f32)
    above = jnp.zeros((count, DY), f32)
    for z in range(DZ):
        value = rows[first : first + count, z, :]
        below = below + sums[own, z] * value
        above = above + sums[own, DZ + z] * value
    extra[0, start : start + count, :] = below
    extra[1, start : start + count, :] = above


def outer_kernel(
    last, end, mid_high, end_high, mid_low, end_low, strips, middle, from_low, from_high, move, gain, w_ref, weight,
    sums, extra_in, *rest,
):
    if last:
        out, extra = rest
    else:
        table, coefs_left, coefs_right, middle_in, out, out_high, out_low, extra, up, down, new_middle = rest
    halo = strips.at[0 if last else 1]
    weight_sum = total_weight(weight)
    zero = jnp.zeros((DZ, 128), f32)

    def halo_rows(slabs):
        return [jnp.concatenate([slabs[2 * row], slabs[2 * row + 1]], axis=1) for row in range(3)]

    low_rows, high_rows = halo_rows(from_low), halo_rows(from_high)
    low_split, high_split = [split(row) for row in low_rows], [split(row) for row in high_rows]
    low_middle, high_middle = zero, zero
    for row in range(3):
        low_middle = add_middle(low_middle, low_rows[row], 13 + row)
        high_middle = add_middle(high_middle, high_rows[row], row)
    sides = [from_low[6], halo[0], halo[1], from_high[6]]
    middles = [low_middle, middle[0], middle[1], high_middle]

    def row_of(which, mid_part, end_part):
        def of(x):
            if x < 0:
                return low_split[x + 3][which]
            if x >= DX:
                return high_split[x - DX][which]
            return end_part[OUTER.index(x)] if x in OUTER else mid_part[x - 3]

        return of

    pairs = [0, 2, DX - 4, DX - 2]
    packed = [zero, zero] if last else [middle_in[0], middle_in[1]]
    for half in range(2):
        around = [two_sides(p, q) if half == 0 else two_sides(q, p) for p, q in zip(sides, middles)]
        edges = []
        for x in pairs:
            group = (x + 13) // 16
            edges.append(edge_window(around[group], around[min(group + 1, 3)], x))
        flux = pair_flux(
            pairs, row_of(0, mid_high, end_high), row_of(1, mid_low, end_low), jnp.concatenate(edges, axis=0), half,
            w_ref,
        )
        part = slice(128 * half, 128 * half + 128)
        for row, x in enumerate(OUTER):
            place = [i for i in range(4) if pairs[i] <= x <= pairs[i] + 1][0]
            new = stepped(
                end[row, :, part], flux(place, x - pairs[place]), move[x, :, part], gain[x, :, part], weight_sum
            )
            out[row, :, part] = new
            if not last:
                out_high[row, :, part], out_low[row, :, part] = split(new)
                slot = 8 * (x % 16)
                source, target = (125, slot) if half == 0 else (0, slot + 4)
                packed[x // 16] = at_lanes(packed[x // 16], new, source, target, 3)
    if last:
        extra[...] = extra_in[...]
        depth_sums(out, sums, extra, 0, 3, 0)
        depth_sums(out, sums, extra, DX - 3, 3, 3)
    else:
        new_middle[0], new_middle[1] = packed
        fill_slabs(lambda row: out[row], up, down)
        lane = lanes()
        low, high = from_low[6], from_high[6]
        beyond = [
            jnp.where(lane < 64, pltpu.roll(high, 96, 1), pltpu.roll(low, 32, 1)),
            jnp.where(lane < 64, high, low),
            jnp.where(lane < 64, pltpu.roll(high, 64, 1), pltpu.roll(low, 64, 1)),
        ]
        taps = [None, None, strip_taps(table, *beyond)]
        for group in range(2):
            flux = extra_in[group] + strip_flux(taps, group)
            left, right = coefs_left[group], coefs_right[group]
            extra[0, group] = stepped(
                halo[group], flux, two_sides(left, right),
                two_sides(pltpu.roll(left, 124, 1), pltpu.roll(right, 4, 1)), weight_sum,
            )
        up[6] = extra[0, 1]
        down[6] = extra[0, 0]


def depth_tables():
    blocks = 4
    stiff = 3.0 * DZ * DZ
    count = DZ * blocks
    diagonal = np.full(count, 1.0 + 2.0 * stiff)
    diagonal[0] = diagonal[-1] = 1.0 + stiff
    fore = diagonal.copy()
    for i in range(1, count):
        fore[i] = diagonal[i] - stiff * stiff / fore[i - 1]
    back = diagonal.copy()
    for i in range(count - 2, -1, -1):
        back[i] = diagonal[i] - stiff * stiff / back[i + 1]

    def from_above(block, other):
        return np.prod(stiff / fore[other * DZ + DZ - 1 : block * DZ])

    def from_below(block, other):
        return np.prod(stiff / back[block * DZ + DZ : other * DZ + 1])

    sums = np.zeros((blocks, 2 * DZ))
    solve = np.zeros((blocks, 2 * DZ))
    reply = np.zeros((blocks, 2 * DZ))
    mix = np.zeros((blocks, 8))
    for block in range(blocks):
        start, end = block * DZ, block * DZ + DZ - 1
        pivots = fore[start : end + 1].copy()
        if block < blocks - 1:
            pivots[-1] = fore[end] - stiff * stiff / back[end + 1]
        for z in range(DZ):
            sums[block, z] = np.prod(stiff / fore[start + z : end])
            sums[block, DZ + z] = np.prod(stiff / back[start + 1 : start + z + 1])
            solve[block, z] = stiff / fore[start + z - 1] if z else 0.0
            solve[block, DZ + z] = 1.0 / pivots[z]
        for side, place in ((0, 0), (1, DZ - 1)):
            value = np.zeros(DZ)
            value[place] = 1.0
            for z in range(1, DZ):
                value[z] += solve[block, z] * value[z - 1]
            value[-1] /= pivots[-1]
            for z in range(DZ - 2, -1, -1):
                value[z] = (value[z] + stiff * value[z + 1]) / pivots[z]
            reply[block, side * DZ : side * DZ + DZ] = 2.0 * value
        partner = block ^ 1
        if block < 2:
            near, far = (1.0, from_above(3, 0) / from_above(3, 1))
            mix[block, 0:2] = (far, near) if block == 0 else (near, far)
            mix[block, 7] = from_below(block, 2)
        else:
            near, far = (1.0, from_below(0, 3) / from_below(0, 2))
            mix[block, 2:4] = (near, far) if block == 2 else (far, near)
            mix[block, 5] = from_above(block, 1)
        if partner < block:
            mix[block, 4] = from_above(block, partner)
        else:
            mix[block, 6] = from_below(block, partner)
    return [jnp.asarray(table, f32) for table in (sums, solve, reply, mix)]


def mix_kernel(own_sums, partner_sums, mix, send, near):
    own = lax.axis_index("gz")
    send[...] = (
        mix[own, 0] * own_sums[0] + mix[own, 1] * partner_sums[0]
        + mix[own, 2] * own_sums[1] + mix[own, 3] * partner_sums[1]
    )
    near[0] = mix[own, 4] * partner_sums[0]
    near[1] = mix[own, 6] * partner_sums[1]


def sweep_kernel(mid, end, solve, sweep, buf):
    for row, x in enumerate(OUTER):
        buf[:, x, :] = end[row]
    for row in range(INNER):
        buf[:, 3 + row, :] = mid[row]
    own = lax.axis_index("gz")
    stiff = 3.0 * DZ * DZ
    value = buf[0]
    sweep[0] = value
    for z in range(1, DZ):
        value = buf[z] + solve[own, z] * value
        sweep[z] = value
    value = value * solve[own, 2 * DZ - 1]
    for z in range(DZ - 1, -1, -1):
        if z < DZ - 1:
            value = (sweep[z] + stiff * value) * solve[own, DZ + z]
        sweep[z] = 2.0 * value - buf[z]


def finish_kernel(swept, near, far, mix, reply, out, buf, out_sem):
    own = lax.axis_index("gz")
    above = near[0] + mix[own, 5] * far[...]
    below = near[1] + mix[own, 7] * far[...]
    parts = range(0, DZ, 16)

    def copy(z):
        part = pl.ds(z, 16)
        return pltpu.make_async_copy(buf.at[part], out.at[part], out_sem.at[z // 16])

    for start in parts:
        for z in range(start, start + 16):
            buf[z] = swept[z] + reply[own, z] * above + reply[own, DZ + z] * below
        copy(start).start()
    for start in parts:
        copy(start).wait()


def shift(value, axis, step):
    count = lax.axis_size(axis)
    return lax.ppermute(value, axis, [(i, (i + step) % count) for i in range(count)])


def local(conc, pit, phase, offsets, damage, weight, diffusivity, rate):
    sums, solve, reply, mix = depth_tables()
    *parts, lasts, firsts, up, down = call(
        first_kernel, "first", PARTS + (PACK, PACK, SLABS, SLABS), [HBM], (VMEM,) * 10,
        [pltpu.VMEM((DX, DZ, DY), f32), SEM((4,))], nbytes=4 << 20, limit=48,
    )(conc)
    left, right = shift(lasts, "gy", 1), shift(firsts, "gy", -1)
    w, move, gain, table, to_high, to_low, middle = call(
        prepare_kernel, "prepare", (struct(9, DY, DY, dtype=bf16), WHOLE, WHOLE, struct(64), PACK, PACK, PACK),
        [SMEM] * 4 + [HBM] * 3 + [VMEM] * 2, (VMEM, VMEM, VMEM, SMEM, VMEM, VMEM, VMEM),
        [pltpu.VMEM((DX, DZ, DY), jnp.int32)] * 3 + [SEM((4,))],
        nbytes=8 << 20, limit=45,
    )(offsets.T, weight, diffusivity, rate, pit, phase, damage, parts[0], parts[1])
    strips, up, down = call(
        join_kernel, "join", (struct(3, 2, DZ, 128), SLABS, SLABS), [VMEM] * 6, (VMEM,) * 3,
    )(left, right, lasts, firsts, up, down)
    for substep in range(2):
        last = substep == 1
        from_low, from_high = shift(up, "gx", 1), shift(down, "gx", -1)
        if not last:
            to_high, to_low, up, down = lax.optimization_barrier((to_high, to_low, up, down))
            coefs = [shift(to_high, "gy", 1), shift(to_low, "gy", -1)]
        mid, end, mid_high, end_high, mid_low, end_low = parts
        tiny = struct(1, 16, 128, dtype=bf16)
        inner_split = (tiny, tiny) if last else (PARTS[2], PARTS[4])
        new_mid, new_mid_high, new_mid_low, more, more_middle = call(
            functools.partial(inner_kernel, last), f"inner{substep}",
            (PARTS[0],) + inner_split + ((struct(2, DX, DY) if last else PACK), struct(1, 8, 128) if last else PACK),
            [VMEM] * 10 + [SMEM] * 3, (VMEM,) * 5, flops=2 * INNER * DZ * DY * 3328, nbytes=12 << 20,
        )(mid, mid_high, end_high, mid_low, end_low, strips, middle, move, gain, w, weight, sums, table)
        args = (end, mid_high, end_high, mid_low, end_low, strips, middle, from_low, from_high, move, gain, w, weight)
        args = args + (sums, more)
        specs = [VMEM] * 12 + [SMEM] * 2 + [VMEM]
        cost = dict(flops=2 * 8 * DZ * DY * 3328, nbytes=6 << 20)
        if last:
            new_end, ends = call(
                functools.partial(outer_kernel, last), "outer1", (PARTS[1], struct(2, DX, DY)), specs, (VMEM,) * 2, **cost
            )(*args)
        else:
            new_end, new_end_high, new_end_low, strips, up, down, middle = call(
                functools.partial(outer_kernel, last), "outer0",
                (PARTS[1], PARTS[3], PARTS[5], struct(1, 2, DZ, 128), SLABS, SLABS, PACK),
                specs + [SMEM, VMEM, VMEM, VMEM], (VMEM,) * 7, **cost,
            )(*args, table, *coefs, more_middle)
            parts = [new_mid, new_end, new_mid_high, new_end_high, new_mid_low, new_end_low]
    partner = lax.ppermute(ends, "gz", [(0, 1), (1, 0), (2, 3), (3, 2)])
    send, near = call(
        mix_kernel, "mix", (struct(DX, DY), struct(2, DX, DY)), [VMEM, VMEM, SMEM], (VMEM,) * 2,
    )(ends, partner, mix)
    send, new_mid, new_end = lax.optimization_barrier((send, new_mid, new_end))
    far = lax.ppermute(send, "gz", [(0, 2), (2, 0), (1, 3), (3, 1)])
    swept = call(
        sweep_kernel, "sweep", struct(DZ, DX, DY), [VMEM, VMEM, SMEM], VMEM, [pltpu.VMEM((DZ, DX, DY), f32)],
        flops=20 << 20, nbytes=4 << 20,
    )(new_mid, new_end, solve)
    return call(
        finish_kernel, "finish", struct(DZ, DX, DY), [VMEM, VMEM, VMEM, SMEM, SMEM], HBM,
        [pltpu.VMEM((DZ, DX, DY), f32), SEM((4,))], nbytes=6 << 20,
    )(swept, near, far, mix, reply)


def solution(mesh):
    block = P("gz", "gx", "gy")
    in_specs = (block, block, block, P(), block, P(), P(), P())
    return jax.shard_map(local, mesh=mesh, in_specs=in_specs, out_specs=block, check_vma=False)
```

```python
import functools

import jax
import jax.numpy as jnp
import numpy as np
from jax import lax
from jax.experimental import pallas as pl
from jax.experimental.pallas import tpu as pltpu
from jax.sharding import PartitionSpec as P

DZ, DX, DY = 64, 32, 256
BONDS = 28
INNER = DX - 6
OUTER = [0, 1, 2, DX - 3, DX - 2, DX - 1]
f32, bf16 = jnp.float32, jnp.bfloat16
lateral_step = 0.02
dissolve_step = 0.25

VMEM = pl.BlockSpec(memory_space=pltpu.VMEM)
SMEM = pl.BlockSpec(memory_space=pltpu.SMEM)
HBM = pl.BlockSpec(memory_space=pltpu.HBM)
ANY = pl.BlockSpec(memory_space=pl.ANY)
SEM = pltpu.SemaphoreType.DMA


def call(kernel, name, out_shape, in_specs, out_specs, scratch=(), flops=0, nbytes=1 << 20, limit=16):
    return pl.pallas_call(
        kernel,
        name=name,
        out_shape=out_shape,
        in_specs=in_specs,
        out_specs=out_specs,
        scratch_shapes=list(scratch),
        cost_estimate=pl.CostEstimate(flops=flops, bytes_accessed=nbytes, transcendentals=0),
        compiler_params=pltpu.CompilerParams(vmem_limit_bytes=limit << 20),
    )


def struct(*dims, dtype=f32):
    return jax.ShapeDtypeStruct(dims, dtype)


PARTS = tuple(struct(n, DZ, DY, dtype=t) for t in (f32, bf16, bf16) for n in (INNER, 6))
PACK = struct(2, DZ, 128)
SLABS = struct(7, DZ, 128)
WHOLE = struct(DX, DZ, DY)


def lanes():
    return lax.broadcasted_iota(jnp.int32, (DZ, 128), 1)


def at_lanes(pack, row, source, target, count):
    lane = lanes()
    moved = pltpu.roll(row, (target - source) % 128, 1)
    return jnp.where((lane >= target) & (lane < target + count), moved, pack)


def two_sides(left, right):
    return jnp.where(lanes() % 8 < 4, left, right)


def by_parity(axis, first, second):
    even = lanes() < jnp.where(lax.axis_index(axis) % 2 == 0, 128, 0)
    return jnp.where(even, first, second), jnp.where(even, second, first)


def split(value):
    high = value.astype(bf16)
    return high, (value - high.astype(f32)).astype(bf16)


def add_middle(pack, row, x):
    slot = 8 * (x % 16)
    pack = at_lanes(pack, row[:, :128], 125, slot, 3)
    return at_lanes(pack, row[:, 128:], 0, slot + 4, 3)


def edge_window(before, after, x):
    slot = 8 * ((x + 13) % 16)
    lane = lanes()
    window = pltpu.roll(jnp.where(lane >= slot, before, after), (128 - slot) % 128, 1)
    high = window.astype(bf16).astype(f32)
    low = pltpu.roll(window - high, 64, 1)
    return jnp.concatenate([jnp.where(lane < 64, high, low).astype(bf16), high.astype(bf16)], axis=1)


def total_weight(weight):
    total = weight[0]
    for bond in range(1, BONDS):
        total = total + weight[bond]
    return total


def prepare_kernel(
    offsets_in, weight_in, diffusivity_in, rate_in, pit, phase, damage, mid, end,
    w_ref, move, gain, table_rows, to_high, to_low, middle,
    pv, hv, dv, offsets, weight, diffusivity, rate, table, sem, scalar_sem,
):
    def copies(group):
        return [
            pltpu.make_async_copy(source.at[:, x, :], target.at[x], sem.at[group])
            for x in range(8 * group, 8 * group + 8)
            for source, target in ((pit, pv), (phase, hv), (damage, dv))
        ]

    scalar_copies = [
        pltpu.make_async_copy(source, target, scalar_sem.at[i])
        for i, (source, target) in enumerate(
            ((offsets_in, offsets), (weight_in, weight), (diffusivity_in, diffusivity), (rate_in, rate))
        )
    ]
    for copy in scalar_copies:
        copy.start()
    for group in range(4):
        for copy in copies(group):
            copy.start()
    for copy in scalar_copies:
        copy.wait()
    for place in range(49):
        table[place] = jnp.float32(0.0)
    for bond in range(BONDS):
        place = (offsets[0, bond] + 3) * 7 + offsets[1, bond] + 3
        table[place] = table[place] + weight[bond]
    for place in range(49):
        table_rows[place : place + 1, :] = jnp.full((1, 128), table[place], f32)
    table_rows[49:50, :] = jnp.full((1, 128), total_weight(weight), f32)
    diff = lax.broadcasted_iota(jnp.int32, (128, 128), 0) - lax.broadcasted_iota(jnp.int32, (128, 128), 1) + 3
    blank = jnp.zeros((128, 128), bf16)
    for start in (0, 4):
        w_ref[start, :128, 128:] = blank
        w_ref[start + 3, 128:, :128] = blank
    for first in range(7):
        band = jnp.zeros((128, 128), f32)
        for second in range(7):
            band = jnp.where(diff == second, table[first * 7 + second], band)
        high, low = split(band)
        for out_row in range(2):
            row = first + out_row
            place = (slice(128 * (row % 2), 128 * (row % 2) + 128), slice(128 * out_row, 128 * out_row + 128))
            w_ref[(row // 2,) + place] = high
            w_ref[(4 + row // 2,) + place] = low
    lane = lax.broadcasted_iota(jnp.int32, (64, DY), 0)
    column = lax.broadcasted_iota(jnp.int32, (64, DY), 1)
    place = lane % 8
    first = lane // 8 - column // 128
    second = jnp.where(place < 4, place, 127 + place) - column % 128
    good = (place != 3) & (place != 7) & (first >= 0) & (first < 7) & (second >= 0) & (second < 7)
    which = jnp.where(good, 7 * first + second, -1)
    edge = jnp.zeros((64, DY), f32)
    for place in range(49):
        edge = jnp.where(which == place, table[place], edge)
    high, low = split(edge)
    for row, value in enumerate((high, high, low, jnp.zeros((64, DY), bf16))):
        w_ref[8, 64 * row : 64 * row + 64, :] = value
    packed = [jnp.zeros((DZ, 128), f32)] * 2
    for x in range(DX):
        packed[x // 16] = add_middle(packed[x // 16], end[OUTER.index(x)] if x in OUTER else mid[x - 3], x)
    middle[0], middle[1] = packed

    def look(ids, values, scale):
        value = jnp.where(ids == 0, values[0] * scale, values[1] * scale)
        return jnp.where(ids < 2, value, jnp.where(ids == 2, values[2] * scale, values[3] * scale))

    for group in range(4):
        for copy in copies(group):
            copy.wait()

        @pl.loop(8 * group, 8 * group + 8)
        def _(x):
            ids = hv[x]
            move[x] = look(ids, diffusivity, lateral_step) * (1.0 + 0.5 * dv[x].astype(f32))
            gain[x] = look(ids, rate, dissolve_step) * pv[x].astype(f32)

        if group % 2 == 0:
            high, low = jnp.zeros((DZ, 128), f32), jnp.zeros((DZ, 128), f32)
        for x in range(8 * group, 8 * group + 8):
            slot = 8 * (x % 16)
            high = at_lanes(high, move[x, :, 128:], 125, slot, 3)
            high = at_lanes(high, gain[x, :, 128:], 125, slot + 4, 3)
            low = at_lanes(low, gain[x, :, :128], 0, slot, 3)
            low = at_lanes(low, move[x, :, :128], 0, slot + 4, 3)
        if group % 2:
            to_high[group // 2], to_low[group // 2] = by_parity("gy", high, low)


def right_side(w_ref):
    high, low = [w_ref[t] for t in range(4)], [w_ref[4 + t] for t in range(4)]
    return jnp.concatenate(high + high + low + [w_ref[8]], axis=0)


def pair_flux(pairs, high_of, low_of, edges, half, w_ref):
    part = slice(128 * half, 128 * half + 128)

    def side(row_of):
        return [jnp.concatenate([row_of(x - 3 + i)[:, part] for x in pairs], axis=0) for i in range(8)]

    high, low = side(high_of), side(low_of)
    left = jnp.concatenate(high + low + high + [edges], axis=1)
    flux = jnp.dot(left, right_side(w_ref), preferred_element_type=f32)

    def of(place, out_row):
        return flux[DZ * place : DZ * place + DZ, 128 * out_row : 128 * out_row + 128]

    return of


def stepped(center, flux, move, gain, weight_sum):
    return center + move * (flux - weight_sum * center) + gain * (1.0 - center)


def first_kernel(conc, mid, end, mid_high, end_high, mid_low, end_low, lasts, firsts, up, down, buf, sem):
    for x in range(DX):
        pltpu.make_async_copy(conc.at[:, x, :], buf.at[x], sem.at[x // 8]).start()
    for group in range(4):
        for x in range(8 * group, 8 * group + 8):
            pltpu.make_async_copy(conc.at[:, x, :], buf.at[x], sem.at[group]).wait()
        if group % 2 == 0:
            high_side, low_side = jnp.zeros((DZ, 128), f32), jnp.zeros((DZ, 128), f32)
        for x in range(8 * group, 8 * group + 8):
            row = buf[x]
            high, low = split(row)
            if x in OUTER:
                place = OUTER.index(x)
                end[place], end_high[place], end_low[place] = row, high, low
            else:
                mid[x - 3], mid_high[x - 3], mid_low[x - 3] = row, high, low
            slot = 8 * (x % 16)
            high_side = at_lanes(high_side, row[:, 128:], 122, slot, 6)
            low_side = at_lanes(low_side, row[:, :128], 0, slot, 6)
        if group % 2:
            lasts[group // 2], firsts[group // 2] = by_parity("gy", high_side, low_side)
    fill_slabs(lambda row: buf[OUTER[row]], up, down)
    down[6] = jnp.zeros((DZ, 128), f32)
    up[6] = jnp.zeros((DZ, 128), f32)


def fill_slabs(row_of, up, down):
    for row in range(3):
        for half in range(2):
            part = slice(128 * half, 128 * half + 128)
            up[2 * row + half], down[2 * row + half] = by_parity("gx", row_of(3 + row)[:, part], row_of(row)[:, part])


def join_kernel(y_first, y_second, own_first, own_second, up_in, down_in, strips, up, down):
    for group in range(2):
        right, left = by_parity("gy", y_first[group], y_second[group])
        lasts, firsts = by_parity("gy", own_first[group], own_second[group])
        strips[0, group] = two_sides(left, pltpu.roll(lasts, 1, 1))
        strips[1, group] = two_sides(pltpu.roll(left, 125, 1), pltpu.roll(right, 4, 1))
        strips[2, group] = two_sides(firsts, pltpu.roll(right, 1, 1))
    for slab in range(6):
        up[slab] = up_in[slab]
        down[slab] = down_in[slab]
    lane = lanes()
    to_next = jnp.where(
        lane >= 104, strips[1, 1],
        jnp.where(lane >= 72, pltpu.roll(strips[0, 1], 96, 1), pltpu.roll(strips[2, 1], 64, 1)),
    )
    to_last = jnp.where(
        lane < 32, strips[1, 0],
        jnp.where(lane < 64, pltpu.roll(strips[0, 0], 32, 1), pltpu.roll(strips[2, 0], 64, 1)),
    )
    up[6], down[6] = by_parity("gx", to_next, to_last)


def strip_taps(table, first, second, third):
    place = lanes() % 4

    def moved(value, step):
        return pltpu.roll(value, step % 128, 1)

    columns = [
        first,
        jnp.where(place < 2, moved(first, -1), moved(second, 2)),
        jnp.where(place < 1, moved(first, -2), moved(second, 1)),
        second,
        jnp.where(place < 2, moved(second, -1), moved(third, 2)),
        jnp.where(place < 1, moved(second, -2), moved(third, 1)),
        third,
    ]
    sums = []
    for a in range(7):
        total = table[7 * a : 7 * a + 1, :] * columns[0]
        for second_index in range(1, 7):
            place = 7 * a + second_index
            total = total + table[place : place + 1, :] * columns[second_index]
        sums.append(total)
    return sums


def strip_flux(taps, group):
    lane = lanes()
    total = jnp.zeros((DZ, 128), f32)
    zero = jnp.zeros((DZ, 128), f32)
    for a in range(7):
        step = 8 * (a - 3)
        own, after, before = (
            zero if taps[g] is None else taps[g][a] for g in (group, (group + 1) % 3, (group + 2) % 3)
        )
        if step == 0:
            total = total + own
        elif step > 0:
            total = total + pltpu.roll(jnp.where(lane >= step, own, after), 128 - step, 1)
        else:
            total = total + pltpu.roll(jnp.where(lane < 128 + step, own, before), -step, 1)
    return total


def inner_kernel(
    last, mid, mid_high, end_high, mid_low, end_low, strips, middle, move, gain, w_ref, sums, table,
    out, out_high, out_low, extra, new_middle,
):
    halo = strips.at[0 if last else 1]
    weight_sum = table[49:50, :]
    pairs = range(3, DX - 3, 2)

    def row_of(mid_part, end_part):
        return lambda x: end_part[OUTER.index(x)] if x in OUTER else mid_part[x - 3]

    packed = [jnp.zeros((DZ, 128), f32)] * 2
    for half in range(2):
        around = [
            two_sides(halo[g], middle[g]) if half == 0 else two_sides(middle[g], halo[g]) for g in range(2)
        ]
        edges = []
        for x in pairs:
            group = (x + 13) // 16 - 1
            edges.append(edge_window(around[group], around[min(group + 1, 1)], x))
        flux = pair_flux(
            pairs, row_of(mid_high, end_high), row_of(mid_low, end_low), jnp.concatenate(edges, axis=0), half, w_ref
        )
        part = slice(128 * half, 128 * half + 128)
        for place, first in enumerate(pairs):
            for out_row in range(2):
                x = first + out_row
                row = x - 3
                new = stepped(mid[row, :, part], flux(place, out_row), move[x, :, part], gain[x, :, part], weight_sum)
                out[row, :, part] = new
                if not last:
                    out_high[row, :, part], out_low[row, :, part] = split(new)
                    slot = 8 * (x % 16)
                    source, target = (125, slot) if half == 0 else (0, slot + 4)
                    packed[x // 16] = at_lanes(packed[x // 16], new, source, target, 3)
    if last:
        extra[...] = jnp.zeros_like(extra)
        depth_sums(out, sums, extra, 3, INNER, 0)
    else:
        new_middle[0], new_middle[1] = packed
        taps = [strip_taps(table, strips[0, g], strips[1, g], strips[2, g]) for g in range(2)] + [None]
        for group in range(2):
            extra[group] = strip_flux(taps, group)


def depth_sums(rows, sums, extra, start, count, first):
    own = lax.axis_index("gz")
    for half in range(2):
        part = slice(128 * half, 128 * half + 128)
        below = jnp.zeros((count, 128), f32)
        above = jnp.zeros((count, 128), f32)
        for z in range(DZ):
            value = rows[first : first + count, z, part]
            below = below + sums[own, z : z + 1, :] * value
            above = above + sums[own, DZ + z : DZ + z + 1, :] * value
        extra[0, start : start + count, part] = below
        extra[1, start : start + count, part] = above


def outer_kernel(
    last, end, mid_high, end_high, mid_low, end_low, strips, middle, x_first, x_second, move, gain, w_ref,
    sums, table, extra_in, *rest,
):
    if last:
        out, extra = rest
    else:
        coefs_first, coefs_second, middle_in, out, out_high, out_low, extra, up, down, new_middle = rest
    halo = strips.at[0 if last else 1]
    weight_sum = table[49:50, :]
    zero = jnp.zeros((DZ, 128), f32)

    def halo_rows(slabs):
        return [jnp.concatenate([slabs[2 * row], slabs[2 * row + 1]], axis=1) for row in range(3)]

    from_high, from_low = zip(*(by_parity("gx", x_first[slab], x_second[slab]) for slab in range(7)))
    low_rows, high_rows = halo_rows(from_low), halo_rows(from_high)
    low_split, high_split = [split(row) for row in low_rows], [split(row) for row in high_rows]
    low_middle, high_middle = zero, zero
    for row in range(3):
        low_middle = add_middle(low_middle, low_rows[row], 13 + row)
        high_middle = add_middle(high_middle, high_rows[row], row)
    sides = [from_low[6], halo[0], halo[1], from_high[6]]
    middles = [low_middle, middle[0], middle[1], high_middle]

    def row_of(which, mid_part, end_part):
        def of(x):
            if x < 0:
                return low_split[x + 3][which]
            if x >= DX:
                return high_split[x - DX][which]
            return end_part[OUTER.index(x)] if x in OUTER else mid_part[x - 3]

        return of

    pairs = [0, 2, DX - 4, DX - 2]
    packed = [zero, zero] if last else [middle_in[0], middle_in[1]]
    for half in range(2):
        around = [two_sides(p, q) if half == 0 else two_sides(q, p) for p, q in zip(sides, middles)]
        edges = []
        for x in pairs:
            group = (x + 13) // 16
            edges.append(edge_window(around[group], around[min(group + 1, 3)], x))
        flux = pair_flux(
            pairs, row_of(0, mid_high, end_high), row_of(1, mid_low, end_low), jnp.concatenate(edges, axis=0), half,
            w_ref,
        )
        part = slice(128 * half, 128 * half + 128)
        for row, x in enumerate(OUTER):
            place = [i for i in range(4) if pairs[i] <= x <= pairs[i] + 1][0]
            new = stepped(
                end[row, :, part], flux(place, x - pairs[place]), move[x, :, part], gain[x, :, part], weight_sum
            )
            out[row, :, part] = new
            if not last:
                out_high[row, :, part], out_low[row, :, part] = split(new)
                slot = 8 * (x % 16)
                source, target = (125, slot) if half == 0 else (0, slot + 4)
                packed[x // 16] = at_lanes(packed[x // 16], new, source, target, 3)
    if last:
        extra[...] = extra_in[...]
        depth_sums(out, sums, extra, 0, 3, 0)
        depth_sums(out, sums, extra, DX - 3, 3, 3)
    else:
        new_middle[0], new_middle[1] = packed
        fill_slabs(lambda row: out[row], up, down)
        lane = lanes()
        low, high = from_low[6], from_high[6]
        beyond = [
            jnp.where(lane < 64, pltpu.roll(high, 96, 1), pltpu.roll(low, 32, 1)),
            jnp.where(lane < 64, high, low),
            jnp.where(lane < 64, pltpu.roll(high, 64, 1), pltpu.roll(low, 64, 1)),
        ]
        taps = [None, None, strip_taps(table, *beyond)]
        for group in range(2):
            flux = extra_in[group] + strip_flux(taps, group)
            right, left = by_parity("gy", coefs_first[group], coefs_second[group])
            extra[0, group] = stepped(
                halo[group], flux, two_sides(left, right),
                two_sides(pltpu.roll(left, 124, 1), pltpu.roll(right, 4, 1)), weight_sum,
            )
        up[6], down[6] = by_parity("gx", extra[0, 1], extra[0, 0])


def depth_tables():
    blocks = 4
    stiff = 3.0 * DZ * DZ
    count = DZ * blocks
    diagonal = np.full(count, 1.0 + 2.0 * stiff)
    diagonal[0] = diagonal[-1] = 1.0 + stiff
    fore = diagonal.copy()
    for i in range(1, count):
        fore[i] = diagonal[i] - stiff * stiff / fore[i - 1]
    back = diagonal.copy()
    for i in range(count - 2, -1, -1):
        back[i] = diagonal[i] - stiff * stiff / back[i + 1]

    def from_above(block, other):
        return np.prod(stiff / fore[other * DZ + DZ - 1 : block * DZ])

    def from_below(block, other):
        return np.prod(stiff / back[block * DZ + DZ : other * DZ + 1])

    sums = np.zeros((blocks, 2 * DZ))
    solve = np.zeros((blocks, 2 * DZ))
    reply = np.zeros((blocks, 2 * DZ))
    mix = np.zeros((blocks, 8))
    for block in range(blocks):
        start, end = block * DZ, block * DZ + DZ - 1
        pivots = fore[start : end + 1].copy()
        if block < blocks - 1:
            pivots[-1] = fore[end] - stiff * stiff / back[end + 1]
        for z in range(DZ):
            sums[block, z] = np.prod(stiff / fore[start + z : end])
            sums[block, DZ + z] = np.prod(stiff / back[start + 1 : start + z + 1])
            solve[block, z] = stiff / fore[start + z - 1] if z else 0.0
            solve[block, DZ + z] = 1.0 / pivots[z]
        for side, place in ((0, 0), (1, DZ - 1)):
            value = np.zeros(DZ)
            value[place] = 1.0
            for z in range(1, DZ):
                value[z] += solve[block, z] * value[z - 1]
            value[-1] /= pivots[-1]
            for z in range(DZ - 2, -1, -1):
                value[z] = (value[z] + stiff * value[z + 1]) / pivots[z]
            reply[block, side * DZ : side * DZ + DZ] = 2.0 * value
        partner = block ^ 1
        if block < 2:
            near, far = (1.0, from_above(3, 0) / from_above(3, 1))
            mix[block, 0:2] = (far, near) if block == 0 else (near, far)
            mix[block, 7] = from_below(block, 2)
        else:
            near, far = (1.0, from_below(0, 3) / from_below(0, 2))
            mix[block, 2:4] = (near, far) if block == 2 else (far, near)
            mix[block, 5] = from_above(block, 1)
        if partner < block:
            mix[block, 4] = from_above(block, partner)
        else:
            mix[block, 6] = from_below(block, partner)
    rows = [jnp.asarray(np.repeat(table[:, :, None], 128, axis=2), f32) for table in (sums, reply)]
    return rows[0], jnp.asarray(solve, f32), rows[1], mix


def own_of(mix, column):
    own = lax.axis_index("gz")
    value = jnp.float32(mix[0, column])
    for block in range(1, 4):
        value = jnp.where(own == block, jnp.float32(mix[block, column]), value)
    return value


def mix_kernel(mix, own_sums, partner_sums, send, near):
    send[...] = (
        own_of(mix, 0) * own_sums[0] + own_of(mix, 1) * partner_sums[0]
        + own_of(mix, 2) * own_sums[1] + own_of(mix, 3) * partner_sums[1]
    )
    near[0] = own_of(mix, 4) * partner_sums[0]
    near[1] = own_of(mix, 6) * partner_sums[1]


def sweep_kernel(mid, end, solve, sweep, buf):
    for row, x in enumerate(OUTER):
        buf[:, x, :] = end[row]
    for row in range(INNER):
        buf[:, 3 + row, :] = mid[row]
    own = lax.axis_index("gz")
    stiff = 3.0 * DZ * DZ
    value = buf[0]
    sweep[0] = value
    for z in range(1, DZ):
        value = buf[z] + solve[own, z] * value
        sweep[z] = value
    value = value * solve[own, 2 * DZ - 1]
    for z in range(DZ - 1, -1, -1):
        if z < DZ - 1:
            value = (sweep[z] + stiff * value) * solve[own, DZ + z]
        sweep[z] = 2.0 * value - buf[z]


def finish_kernel(mix, swept, near, far, reply, out, buf, out_sem):
    own = lax.axis_index("gz")
    above = near[0] + own_of(mix, 5) * far[...]
    below = near[1] + own_of(mix, 7) * far[...]
    size = 8

    def copy(z):
        part = pl.ds(z, size)
        return pltpu.make_async_copy(buf.at[part], out.at[part], out_sem.at[z // size])

    for start in range(0, DZ, size):
        for z in range(start, start + size):
            for half in range(2):
                part = slice(128 * half, 128 * half + 128)
                buf[z, :, part] = (
                    swept[z, :, part] + reply[own, z : z + 1, :] * above[:, part]
                    + reply[own, DZ + z : DZ + z + 1, :] * below[:, part]
                )
        copy(start).start()
    for start in range(0, DZ, size):
        copy(start).wait()


def swaps(first, second, axis):
    count = lax.axis_size(axis)
    moved = []
    for start, value in ((0, first), (1, second)):
        pairs = [(i, (i + 1) % count) for i in range(start, count, 2)]
        moved.append(lax.ppermute(value, axis, pairs + [(target, source) for source, target in pairs]))
    return moved


def local(conc, pit, phase, offsets, damage, weight, diffusivity, rate):
    sums, solve, reply, mix = depth_tables()
    *parts, lasts, firsts, up, down = call(
        first_kernel, "first", PARTS + (PACK, PACK, SLABS, SLABS), [HBM], (VMEM,) * 10,
        [pltpu.VMEM((DX, DZ, DY), f32), SEM((4,))], nbytes=4 << 20, limit=48,
    )(conc)
    left, right = swaps(lasts, firsts, "gy")
    w, move, gain, table, to_high, to_low, middle = call(
        prepare_kernel, "prepare", (struct(9, DY, DY, dtype=bf16), WHOLE, WHOLE, struct(56, 128), PACK, PACK, PACK),
        [ANY] * 4 + [HBM] * 3 + [VMEM] * 2, (VMEM,) * 7,
        [pltpu.VMEM((DX, DZ, DY), jnp.int32)] * 3
        + [pltpu.SMEM((2, BONDS), jnp.int32), pltpu.SMEM((BONDS,), f32), pltpu.SMEM((4,), f32), pltpu.SMEM((4,), f32)]
        + [pltpu.SMEM((64,), f32), SEM((4,)), SEM((4,))],
        nbytes=8 << 20, limit=45,
    )(offsets.T, weight, diffusivity, rate, pit, phase, damage, parts[0], parts[1])
    strips, up, down = call(
        join_kernel, "join", (struct(3, 2, DZ, 128), SLABS, SLABS), [VMEM] * 6, (VMEM,) * 3,
    )(left, right, lasts, firsts, up, down)
    for substep in range(2):
        last = substep == 1
        x_first, x_second = swaps(up, down, "gx")
        if not last:
            to_high, to_low, up, down = lax.optimization_barrier((to_high, to_low, up, down))
            coefs = swaps(to_high, to_low, "gy")
        mid, end, mid_high, end_high, mid_low, end_low = parts
        tiny = struct(1, 16, 128, dtype=bf16)
        inner_split = (tiny, tiny) if last else (PARTS[2], PARTS[4])
        new_mid, new_mid_high, new_mid_low, more, more_middle = call(
            functools.partial(inner_kernel, last), f"inner{substep}",
            (PARTS[0],) + inner_split + ((struct(2, DX, DY) if last else PACK), struct(1, 8, 128) if last else PACK),
            [VMEM] * 12, (VMEM,) * 5, flops=2 * INNER * DZ * DY * 3328, nbytes=12 << 20,
        )(mid, mid_high, end_high, mid_low, end_low, strips, middle, move, gain, w, sums, table)
        args = (end, mid_high, end_high, mid_low, end_low, strips, middle, x_first, x_second, move, gain, w)
        args = args + (sums, table, more)
        specs = [VMEM] * 15
        cost = dict(flops=2 * 8 * DZ * DY * 3328, nbytes=6 << 20)
        if last:
            new_end, ends = call(
                functools.partial(outer_kernel, last), "outer1", (PARTS[1], struct(2, DX, DY)), specs, (VMEM,) * 2, **cost
            )(*args)
        else:
            new_end, new_end_high, new_end_low, strips, up, down, middle = call(
                functools.partial(outer_kernel, last), "outer0",
                (PARTS[1], PARTS[3], PARTS[5], struct(1, 2, DZ, 128), SLABS, SLABS, PACK),
                specs + [VMEM] * 3, (VMEM,) * 7, **cost,
            )(*args, *coefs, more_middle)
            parts = [new_mid, new_end, new_mid_high, new_end_high, new_mid_low, new_end_low]
    partner = lax.ppermute(ends, "gz", [(0, 1), (1, 0), (2, 3), (3, 2)])
    send, near = call(
        functools.partial(mix_kernel, mix), "mix", (struct(DX, DY), struct(2, DX, DY)), [VMEM, VMEM], (VMEM,) * 2,
    )(ends, partner)
    send, new_mid, new_end = lax.optimization_barrier((send, new_mid, new_end))
    far = lax.ppermute(send, "gz", [(0, 2), (2, 0), (1, 3), (3, 1)])
    swept = call(
        sweep_kernel, "sweep", struct(DZ, DX, DY), [VMEM, VMEM, SMEM], VMEM, [pltpu.VMEM((DZ, DX, DY), f32)],
        flops=20 << 20, nbytes=4 << 20,
    )(new_mid, new_end, solve)
    return call(
        functools.partial(finish_kernel, mix), "finish", struct(DZ, DX, DY), [VMEM] * 4, HBM,
        [pltpu.VMEM((DZ, DX, DY), f32), SEM((8,))], nbytes=6 << 20,
    )(swept, near, far, reply)


def solution(mesh):
    block = P("gz", "gx", "gy")
    in_specs = (block, block, block, P(), block, P(), P(), P())
    return jax.shard_map(local, mesh=mesh, in_specs=in_specs, out_specs=block, check_vma=False)
```

```python
import functools

import jax
import jax.numpy as jnp
import numpy as np
from jax import lax
from jax.experimental import pallas as pl
from jax.experimental.pallas import tpu as pltpu
from jax.sharding import PartitionSpec as P

DZ, DX, DY = 64, 32, 256
BONDS = 28
INNER = DX - 6
OUTER = [0, 1, 2, DX - 3, DX - 2, DX - 1]
f32, bf16 = jnp.float32, jnp.bfloat16
lateral_step = 0.02
dissolve_step = 0.25

VMEM = pl.BlockSpec(memory_space=pltpu.VMEM)
SMEM = pl.BlockSpec(memory_space=pltpu.SMEM)
HBM = pl.BlockSpec(memory_space=pltpu.HBM)
ANY = pl.BlockSpec(memory_space=pl.ANY)
SEM = pltpu.SemaphoreType.DMA


def call(kernel, name, out_shape, in_specs, out_specs, scratch=(), flops=0, nbytes=1 << 20, limit=16):
    return pl.pallas_call(
        kernel,
        name=name,
        out_shape=out_shape,
        in_specs=in_specs,
        out_specs=out_specs,
        scratch_shapes=list(scratch),
        cost_estimate=pl.CostEstimate(flops=flops, bytes_accessed=nbytes, transcendentals=0),
        compiler_params=pltpu.CompilerParams(vmem_limit_bytes=limit << 20),
    )


def struct(*dims, dtype=f32):
    return jax.ShapeDtypeStruct(dims, dtype)


PARTS = tuple(struct(n, DZ, DY, dtype=t) for t in (f32, bf16, bf16) for n in (INNER, 6))
PACK = struct(2, DZ, 128)
SLABS = struct(6 * DZ, 128)
TAIL = DZ // 4
WHOLE = struct(DX, DZ, DY)


def lanes():
    return lax.broadcasted_iota(jnp.int32, (DZ, 128), 1)


def at_lanes(pack, row, source, target, count):
    lane = lanes()
    moved = pltpu.roll(row, (target - source) % 128, 1)
    return jnp.where((lane >= target) & (lane < target + count), moved, pack)


def two_sides(left, right):
    return jnp.where(lanes() % 8 < 4, left, right)


def by_parity(axis, first, second):
    lane = lax.broadcasted_iota(jnp.int32, first.shape, 1)
    odd = lane < jnp.where(lax.axis_index(axis) % 2 == 1, 128, 0)
    return jnp.where(odd, first, second), jnp.where(odd, second, first)


def fold(strip, start):
    lane = lax.broadcasted_iota(jnp.int32, (TAIL, 128), 1)
    folded = jnp.zeros((TAIL, 128), f32)
    for part in range(4):
        moved = pltpu.roll(strip[TAIL * part : TAIL * part + TAIL], (32 * part - start) % 128, 1)
        folded = jnp.where(lane // 32 == part, moved, folded)
    return folded


def unfold(folded, start):
    return jnp.concatenate([pltpu.roll(folded, (start - 32 * part) % 128, 1) for part in range(4)], axis=0)


def slab(index):
    return pl.ds(DZ * index, DZ)


def tail(index):
    return pl.ds(6 * DZ + TAIL * index, TAIL)


def split(value):
    high = value.astype(bf16)
    return high, (value - high.astype(f32)).astype(bf16)


def add_middle(pack, row, x):
    slot = 8 * (x % 16)
    pack = at_lanes(pack, row[:, :128], 125, slot, 3)
    return at_lanes(pack, row[:, 128:], 0, slot + 4, 3)


def edge_window(before, after, x):
    slot = 8 * ((x + 13) % 16)
    lane = lanes()
    window = pltpu.roll(jnp.where(lane >= slot, before, after), (128 - slot) % 128, 1)
    high = window.astype(bf16).astype(f32)
    low = pltpu.roll(window - high, 64, 1)
    return jnp.concatenate([jnp.where(lane < 64, high, low).astype(bf16), high.astype(bf16)], axis=1)


def total_weight(weight):
    total = weight[0]
    for bond in range(1, BONDS):
        total = total + weight[bond]
    return total


def prepare_kernel(
    offsets_in, weight_in, diffusivity_in, rate_in, pit, phase, damage,
    w_ref, move, gain, table_rows, to_high, to_low,
    pv, hv, dv, offsets, weight, diffusivity, rate, table, sem, scalar_sem,
):
    def copies(group):
        return [
            pltpu.make_async_copy(source.at[:, x, :], target.at[x], sem.at[group])
            for x in range(8 * group, 8 * group + 8)
            for source, target in ((pit, pv), (phase, hv), (damage, dv))
        ]

    scalar_copies = [
        pltpu.make_async_copy(source, target, scalar_sem.at[i])
        for i, (source, target) in enumerate(
            ((offsets_in, offsets), (weight_in, weight), (diffusivity_in, diffusivity), (rate_in, rate))
        )
    ]
    for copy in scalar_copies:
        copy.start()
    for group in range(4):
        for copy in copies(group):
            copy.start()
    for copy in scalar_copies:
        copy.wait()
    for place in range(49):
        table[place] = jnp.float32(0.0)
    for bond in range(BONDS):
        place = (offsets[0, bond] + 3) * 7 + offsets[1, bond] + 3
        table[place] = table[place] + weight[bond]
    for place in range(49):
        table_rows[place : place + 1, :] = jnp.full((1, 128), table[place], f32)
    table_rows[49:50, :] = jnp.full((1, 128), total_weight(weight), f32)
    diff = lax.broadcasted_iota(jnp.int32, (128, 128), 0) - lax.broadcasted_iota(jnp.int32, (128, 128), 1) + 3
    blank = jnp.zeros((128, 128), bf16)
    for start in (0, 4):
        w_ref[start, :128, 128:] = blank
        w_ref[start + 3, 128:, :128] = blank
    for first in range(7):
        band = jnp.zeros((128, 128), f32)
        for second in range(7):
            band = jnp.where(diff == second, table[first * 7 + second], band)
        high, low = split(band)
        for out_row in range(2):
            row = first + out_row
            place = (slice(128 * (row % 2), 128 * (row % 2) + 128), slice(128 * out_row, 128 * out_row + 128))
            w_ref[(row // 2,) + place] = high
            w_ref[(4 + row // 2,) + place] = low
    lane = lax.broadcasted_iota(jnp.int32, (64, DY), 0)
    column = lax.broadcasted_iota(jnp.int32, (64, DY), 1)
    place = lane % 8
    first = lane // 8 - column // 128
    second = jnp.where(place < 4, place, 127 + place) - column % 128
    good = (place != 3) & (place != 7) & (first >= 0) & (first < 7) & (second >= 0) & (second < 7)
    which = jnp.where(good, 7 * first + second, -1)
    edge = jnp.zeros((64, DY), f32)
    for place in range(49):
        edge = jnp.where(which == place, table[place], edge)
    high, low = split(edge)
    for row, value in enumerate((high, high, low, jnp.zeros((64, DY), bf16))):
        w_ref[8, 64 * row : 64 * row + 64, :] = value
    def look(ids, values, scale):
        value = jnp.where(ids == 0, values[0] * scale, values[1] * scale)
        return jnp.where(ids < 2, value, jnp.where(ids == 2, values[2] * scale, values[3] * scale))

    for group in range(4):
        for copy in copies(group):
            copy.wait()

        @pl.loop(8 * group, 8 * group + 8)
        def _(x):
            ids = hv[x]
            move[x] = look(ids, diffusivity, lateral_step) * (1.0 + 0.5 * dv[x].astype(f32))
            gain[x] = look(ids, rate, dissolve_step) * pv[x].astype(f32)

        if group % 2 == 0:
            high, low = jnp.zeros((DZ, 128), f32), jnp.zeros((DZ, 128), f32)
        for x in range(8 * group, 8 * group + 8):
            slot = 8 * (x % 16)
            high = at_lanes(high, move[x, :, 128:], 125, slot, 3)
            high = at_lanes(high, gain[x, :, 128:], 125, slot + 4, 3)
            low = at_lanes(low, gain[x, :, :128], 0, slot, 3)
            low = at_lanes(low, move[x, :, :128], 0, slot + 4, 3)
        if group % 2:
            to_high[group // 2], to_low[group // 2] = by_parity("gy", high, low)


def right_side(w_ref):
    high, low = [w_ref[t] for t in range(4)], [w_ref[4 + t] for t in range(4)]
    return jnp.concatenate(high + high + low + [w_ref[8]], axis=0)


def pair_flux(pairs, high_of, low_of, edges, half, w_ref):
    part = slice(128 * half, 128 * half + 128)

    def side(row_of):
        return [jnp.concatenate([row_of(x - 3 + i)[:, part] for x in pairs], axis=0) for i in range(8)]

    high, low = side(high_of), side(low_of)
    left = jnp.concatenate(high + low + high + [edges], axis=1)
    flux = jnp.dot(left, right_side(w_ref), preferred_element_type=f32)

    def of(place, out_row):
        return flux[DZ * place : DZ * place + DZ, 128 * out_row : 128 * out_row + 128]

    return of


def stepped(center, flux, move, gain, weight_sum):
    return center + move * (flux - weight_sum * center) + gain * (1.0 - center)


def first_kernel(conc, mid, end, lasts, firsts, up, down, sem):
    def row_ref(x):
        return end.at[OUTER.index(x)] if x in OUTER else mid.at[x - 3]

    for x in range(DX):
        pltpu.make_async_copy(conc.at[:, x, :], row_ref(x), sem.at[x // 8]).start()
    for group in range(4):
        for x in range(8 * group, 8 * group + 8):
            pltpu.make_async_copy(conc.at[:, x, :], row_ref(x), sem.at[group]).wait()
        if group % 2 == 0:
            high_side, low_side = jnp.zeros((DZ, 128), f32), jnp.zeros((DZ, 128), f32)
        for x in range(8 * group, 8 * group + 8):
            slot = 8 * (x % 16)
            row = row_ref(x)
            high_side = at_lanes(high_side, row[:, 128:], 122, slot, 6)
            low_side = at_lanes(low_side, row[:, :128], 0, slot, 6)
        if group % 2:
            lasts[group // 2], firsts[group // 2] = by_parity("gy", high_side, low_side)
    fill_slabs(lambda row: end[row], up, down)


def fill_slabs(row_of, up, down):
    for row in range(3):
        for half in range(2):
            part = slice(128 * half, 128 * half + 128)
            place = slab(2 * row + half)
            up[place], down[place] = by_parity("gx", row_of(3 + row)[:, part], row_of(row)[:, part])


def join_kernel(y_first, y_second, own_first, own_second, up_in, down_in, strips, up, down):
    for group in range(2):
        right, left = by_parity("gy", y_first[group], y_second[group])
        lasts, firsts = by_parity("gy", own_first[group], own_second[group])
        strips[0, group] = two_sides(left, pltpu.roll(lasts, 1, 1))
        strips[1, group] = two_sides(pltpu.roll(left, 125, 1), pltpu.roll(right, 4, 1))
        strips[2, group] = two_sides(firsts, pltpu.roll(right, 1, 1))
    for index in range(6):
        up[slab(index)] = up_in[slab(index)]
        down[slab(index)] = down_in[slab(index)]
    for index in range(3):
        up[tail(index)], down[tail(index)] = by_parity("gx", fold(strips[index, 1], 96), fold(strips[index, 0], 0))


def strip_taps(table, first, second, third):
    place = lanes() % 4

    def moved(value, step):
        return pltpu.roll(value, step % 128, 1)

    columns = [
        first,
        jnp.where(place < 2, moved(first, -1), moved(second, 2)),
        jnp.where(place < 1, moved(first, -2), moved(second, 1)),
        second,
        jnp.where(place < 2, moved(second, -1), moved(third, 2)),
        jnp.where(place < 1, moved(second, -2), moved(third, 1)),
        third,
    ]
    sums = []
    for a in range(7):
        total = table[7 * a : 7 * a + 1, :] * columns[0]
        for second_index in range(1, 7):
            place = 7 * a + second_index
            total = total + table[place : place + 1, :] * columns[second_index]
        sums.append(total)
    return sums


def strip_flux(taps, group):
    lane = lanes()
    total = jnp.zeros((DZ, 128), f32)
    zero = jnp.zeros((DZ, 128), f32)
    for a in range(7):
        step = 8 * (a - 3)
        own, after, before = (
            zero if taps[g] is None else taps[g][a] for g in (group, (group + 1) % 3, (group + 2) % 3)
        )
        if step == 0:
            total = total + own
        elif step > 0:
            total = total + pltpu.roll(jnp.where(lane >= step, own, after), 128 - step, 1)
        else:
            total = total + pltpu.roll(jnp.where(lane < 128 + step, own, before), -step, 1)
    return total


def inner_kernel(last, mid, *rest):
    if last:
        mid_high, end_high, mid_low, end_low, strips, middle, move, gain, w_ref, sums, table, out, extra = rest
    else:
        (
            end, strips, move, gain, w_ref, table,
            out, out_high, out_low, extra, new_middle, mid_high, end_high, mid_low, end_low, middle,
        ) = rest
        packed = [jnp.zeros((DZ, 128), f32)] * 2
        for x in range(DX):
            if x in OUTER:
                place = OUTER.index(x)
                row = end[place]
                end_high[place], end_low[place] = split(row)
            else:
                row = mid[x - 3]
                mid_high[x - 3], mid_low[x - 3] = split(row)
            packed[x // 16] = add_middle(packed[x // 16], row, x)
        middle[0], middle[1] = packed
    halo = strips.at[0 if last else 1]
    weight_sum = table[49:50, :]
    pairs = range(3, DX - 3, 2)

    def row_of(mid_part, end_part):
        return lambda x: end_part[OUTER.index(x)] if x in OUTER else mid_part[x - 3]

    packed = [jnp.zeros((DZ, 128), f32)] * 2
    for half in range(2):
        around = [
            two_sides(halo[g], middle[g]) if half == 0 else two_sides(middle[g], halo[g]) for g in range(2)
        ]
        edges = []
        for x in pairs:
            group = (x + 13) // 16 - 1
            edges.append(edge_window(around[group], around[min(group + 1, 1)], x))
        flux = pair_flux(
            pairs, row_of(mid_high, end_high), row_of(mid_low, end_low), jnp.concatenate(edges, axis=0), half, w_ref
        )
        part = slice(128 * half, 128 * half + 128)
        for place, first in enumerate(pairs):
            for out_row in range(2):
                x = first + out_row
                row = x - 3
                new = stepped(mid[row, :, part], flux(place, out_row), move[x, :, part], gain[x, :, part], weight_sum)
                out[row, :, part] = new
                if not last:
                    out_high[row, :, part], out_low[row, :, part] = split(new)
                    slot = 8 * (x % 16)
                    source, target = (125, slot) if half == 0 else (0, slot + 4)
                    packed[x // 16] = at_lanes(packed[x // 16], new, source, target, 3)
    if last:
        extra[...] = jnp.zeros_like(extra)
        depth_sums(out, sums, extra, 3, INNER, 0)
    else:
        new_middle[0], new_middle[1] = packed
        taps = [strip_taps(table, strips[0, g], strips[1, g], strips[2, g]) for g in range(2)] + [None]
        for group in range(2):
            extra[group] = strip_flux(taps, group)


def depth_sums(rows, sums, extra, start, count, first):
    own = lax.axis_index("gz")
    for half in range(2):
        part = slice(128 * half, 128 * half + 128)
        below = jnp.zeros((count, 128), f32)
        above = jnp.zeros((count, 128), f32)
        for z in range(DZ):
            value = rows[first : first + count, z, part]
            below = below + sums[own, z : z + 1, :] * value
            above = above + sums[own, DZ + z : DZ + z + 1, :] * value
        extra[0, start : start + count, part] = below
        extra[1, start : start + count, part] = above


def outer_kernel(
    last, end, mid_high, end_high, mid_low, end_low, strips, middle, x_first, x_second, move, gain, w_ref,
    sums, table, extra_in, *rest,
):
    if last:
        out, extra = rest
    else:
        coefs_first, coefs_second, middle_in, out, out_high, out_low, extra, up, down, new_middle = rest
    halo = strips.at[0 if last else 1]
    weight_sum = table[49:50, :]
    zero = jnp.zeros((DZ, 128), f32)

    def halo_rows(slabs):
        return [jnp.concatenate([slabs[2 * row], slabs[2 * row + 1]], axis=1) for row in range(3)]

    def received(place):
        return by_parity("gx", x_first[place], x_second[place])

    from_high, from_low = zip(*(received(slab(index)) for index in range(6)))
    tails = [received(tail(index)) for index in range(1 if last else 3)]
    high_strips, low_strips = [unfold(high, 0) for high, _ in tails], [unfold(low, 96) for _, low in tails]
    low_rows, high_rows = halo_rows(from_low), halo_rows(from_high)
    low_split, high_split = [split(row) for row in low_rows], [split(row) for row in high_rows]
    low_middle, high_middle = zero, zero
    for row in range(3):
        low_middle = add_middle(low_middle, low_rows[row], 13 + row)
        high_middle = add_middle(high_middle, high_rows[row], row)
    here = 0 if last else 1
    sides = [low_strips[here], halo[0], halo[1], high_strips[here]]
    middles = [low_middle, middle[0], middle[1], high_middle]

    def row_of(which, mid_part, end_part):
        def of(x):
            if x < 0:
                return low_split[x + 3][which]
            if x >= DX:
                return high_split[x - DX][which]
            return end_part[OUTER.index(x)] if x in OUTER else mid_part[x - 3]

        return of

    pairs = [0, 2, DX - 4, DX - 2]
    packed = [zero, zero] if last else [middle_in[0], middle_in[1]]
    for half in range(2):
        around = [two_sides(p, q) if half == 0 else two_sides(q, p) for p, q in zip(sides, middles)]
        edges = []
        for x in pairs:
            group = (x + 13) // 16
            edges.append(edge_window(around[group], around[min(group + 1, 3)], x))
        flux = pair_flux(
            pairs, row_of(0, mid_high, end_high), row_of(1, mid_low, end_low), jnp.concatenate(edges, axis=0), half,
            w_ref,
        )
        part = slice(128 * half, 128 * half + 128)
        for row, x in enumerate(OUTER):
            place = [i for i in range(4) if pairs[i] <= x <= pairs[i] + 1][0]
            new = stepped(
                end[row, :, part], flux(place, x - pairs[place]), move[x, :, part], gain[x, :, part], weight_sum
            )
            out[row, :, part] = new
            if not last:
                out_high[row, :, part], out_low[row, :, part] = split(new)
                slot = 8 * (x % 16)
                source, target = (125, slot) if half == 0 else (0, slot + 4)
                packed[x // 16] = at_lanes(packed[x // 16], new, source, target, 3)
    if last:
        extra[...] = extra_in[...]
        depth_sums(out, sums, extra, 0, 3, 0)
        depth_sums(out, sums, extra, DX - 3, 3, 3)
    else:
        new_middle[0], new_middle[1] = packed
        fill_slabs(lambda row: out[row], up, down)
        lane = lanes()
        beyond = [jnp.where(lane < 64, high, low) for high, low in zip(high_strips, low_strips)]
        taps = [None, None, strip_taps(table, *beyond)]
        for group in range(2):
            flux = extra_in[group] + strip_flux(taps, group)
            right, left = by_parity("gy", coefs_first[group], coefs_second[group])
            extra[0, group] = stepped(
                halo[group], flux, two_sides(left, right),
                two_sides(pltpu.roll(left, 124, 1), pltpu.roll(right, 4, 1)), weight_sum,
            )
        up[tail(0)], down[tail(0)] = by_parity("gx", fold(extra[0, 1], 96), fold(extra[0, 0], 0))


def depth_tables():
    blocks = 4
    stiff = 3.0 * DZ * DZ
    count = DZ * blocks
    diagonal = np.full(count, 1.0 + 2.0 * stiff)
    diagonal[0] = diagonal[-1] = 1.0 + stiff
    fore = diagonal.copy()
    for i in range(1, count):
        fore[i] = diagonal[i] - stiff * stiff / fore[i - 1]
    back = diagonal.copy()
    for i in range(count - 2, -1, -1):
        back[i] = diagonal[i] - stiff * stiff / back[i + 1]

    def from_above(block, other):
        return np.prod(stiff / fore[other * DZ + DZ - 1 : block * DZ])

    def from_below(block, other):
        return np.prod(stiff / back[block * DZ + DZ : other * DZ + 1])

    sums = np.zeros((blocks, 2 * DZ))
    solve = np.zeros((blocks, 2 * DZ))
    reply = np.zeros((blocks, 2 * DZ))
    mix = np.zeros((blocks, 8))
    for block in range(blocks):
        start, end = block * DZ, block * DZ + DZ - 1
        pivots = fore[start : end + 1].copy()
        if block < blocks - 1:
            pivots[-1] = fore[end] - stiff * stiff / back[end + 1]
        for z in range(DZ):
            sums[block, z] = np.prod(stiff / fore[start + z : end])
            sums[block, DZ + z] = np.prod(stiff / back[start + 1 : start + z + 1])
            solve[block, z] = stiff / fore[start + z - 1] if z else 0.0
            solve[block, DZ + z] = 1.0 / pivots[z]
        for side, place in ((0, 0), (1, DZ - 1)):
            value = np.zeros(DZ)
            value[place] = 1.0
            for z in range(1, DZ):
                value[z] += solve[block, z] * value[z - 1]
            value[-1] /= pivots[-1]
            for z in range(DZ - 2, -1, -1):
                value[z] = (value[z] + stiff * value[z + 1]) / pivots[z]
            reply[block, side * DZ : side * DZ + DZ] = 2.0 * value
        partner = block ^ 1
        if block < 2:
            near, far = (1.0, from_above(3, 0) / from_above(3, 1))
            mix[block, 0:2] = (far, near) if block == 0 else (near, far)
            mix[block, 7] = from_below(block, 2)
        else:
            near, far = (1.0, from_below(0, 3) / from_below(0, 2))
            mix[block, 2:4] = (near, far) if block == 2 else (far, near)
            mix[block, 5] = from_above(block, 1)
        if partner < block:
            mix[block, 4] = from_above(block, partner)
        else:
            mix[block, 6] = from_below(block, partner)
    rows = [jnp.asarray(np.repeat(table[:, :, None], 128, axis=2), f32) for table in (sums, reply)]
    return rows[0], jnp.asarray(solve, f32), rows[1], mix


def own_of(mix, column):
    own = lax.axis_index("gz")
    value = jnp.float32(mix[0, column])
    for block in range(1, 4):
        value = jnp.where(own == block, jnp.float32(mix[block, column]), value)
    return value


def mix_kernel(mix, own_sums, partner_sums, send, near):
    send[...] = (
        own_of(mix, 0) * own_sums[0] + own_of(mix, 1) * partner_sums[0]
        + own_of(mix, 2) * own_sums[1] + own_of(mix, 3) * partner_sums[1]
    )
    near[0] = own_of(mix, 4) * partner_sums[0]
    near[1] = own_of(mix, 6) * partner_sums[1]


def sweep_kernel(mid, end, solve, sweep, buf):
    for row, x in enumerate(OUTER):
        buf[:, x, :] = end[row]
    for row in range(INNER):
        buf[:, 3 + row, :] = mid[row]
    own = lax.axis_index("gz")
    stiff = 3.0 * DZ * DZ
    value = buf[0]
    sweep[0] = value
    for z in range(1, DZ):
        value = buf[z] + solve[own, z] * value
        sweep[z] = value
    value = value * solve[own, 2 * DZ - 1]
    for z in range(DZ - 1, -1, -1):
        if z < DZ - 1:
            value = (sweep[z] + stiff * value) * solve[own, DZ + z]
        sweep[z] = 2.0 * value - buf[z]


def finish_kernel(mix, swept, near, far, reply, out, buf, out_sem):
    own = lax.axis_index("gz")
    above = near[0] + own_of(mix, 5) * far[...]
    below = near[1] + own_of(mix, 7) * far[...]
    size = 8

    def copy(z):
        part = pl.ds(z, size)
        return pltpu.make_async_copy(buf.at[part], out.at[part], out_sem.at[z // size])

    for start in range(0, DZ, size):
        for z in range(start, start + size):
            for half in range(2):
                part = slice(128 * half, 128 * half + 128)
                buf[z, :, part] = (
                    swept[z, :, part] + reply[own, z : z + 1, :] * above[:, part]
                    + reply[own, DZ + z : DZ + z + 1, :] * below[:, part]
                )
        copy(start).start()
    for start in range(0, DZ, size):
        copy(start).wait()


def swaps(first, second, axis):
    count = lax.axis_size(axis)
    moved = []
    for start, value in ((1, first), (0, second)):
        pairs = [(i, (i + 1) % count) for i in range(start, count, 2)]
        moved.append(lax.ppermute(value, axis, pairs + [(target, source) for source, target in pairs]))
    return moved


def local(conc, pit, phase, offsets, damage, weight, diffusivity, rate):
    sums, solve, reply, mix = depth_tables()
    mid, end, lasts, firsts, up, down = call(
        first_kernel, "first", PARTS[:2] + (PACK, PACK, SLABS, SLABS), [HBM], (VMEM,) * 6, [SEM((4,))],
        nbytes=4 << 20, limit=51,
    )(conc)
    left, right = swaps(lasts, firsts, "gy")
    w, move, gain, table, to_high, to_low = call(
        prepare_kernel, "prepare", (struct(9, DY, DY, dtype=bf16), WHOLE, WHOLE, struct(56, 128), PACK, PACK),
        [ANY] * 4 + [HBM] * 3, (VMEM,) * 6,
        [pltpu.VMEM((DX, DZ, DY), jnp.int32)] * 3
        + [pltpu.SMEM((2, BONDS), jnp.int32), pltpu.SMEM((BONDS,), f32), pltpu.SMEM((4,), f32), pltpu.SMEM((4,), f32)]
        + [pltpu.SMEM((64,), f32), SEM((4,)), SEM((4,))],
        nbytes=8 << 20, limit=47,
    )(offsets.T, weight, diffusivity, rate, pit, phase, damage)
    strips, up, down = call(
        join_kernel, "join", (struct(3, 2, DZ, 128), struct(6 * DZ + 3 * TAIL, 128), struct(6 * DZ + 3 * TAIL, 128)), [VMEM] * 6, (VMEM,) * 3,
    )(left, right, lasts, firsts, up, down)
    inner_cost = dict(flops=2 * INNER * DZ * DY * 3328, nbytes=12 << 20)
    outer_cost = dict(flops=2 * 8 * DZ * DY * 3328, nbytes=6 << 20)

    x_first, x_second = swaps(up, down, "gx")
    to_high, to_low, up, down = lax.optimization_barrier((to_high, to_low, up, down))
    coefs = swaps(to_high, to_low, "gy")
    new_mid, new_mid_high, new_mid_low, flux, new_middle, mid_high, end_high, mid_low, end_low, middle = call(
        functools.partial(inner_kernel, False), "inner0",
        (PARTS[0], PARTS[2], PARTS[4], PACK, PACK, PARTS[2], PARTS[3], PARTS[4], PARTS[5], PACK),
        [VMEM] * 7, (VMEM,) * 10, **inner_cost,
    )(mid, end, strips, move, gain, w, table)
    new_end, new_end_high, new_end_low, strips, up, down, new_middle = call(
        functools.partial(outer_kernel, False), "outer0",
        (PARTS[1], PARTS[3], PARTS[5], struct(1, 2, DZ, 128), struct(6 * DZ + TAIL, 128), struct(6 * DZ + TAIL, 128), PACK),
        [VMEM] * 18, (VMEM,) * 7, **outer_cost,
    )(
        end, mid_high, end_high, mid_low, end_low, strips, middle, x_first, x_second, move, gain, w, sums, table, flux,
        *coefs, new_middle,
    )

    x_first, x_second = swaps(up, down, "gx")
    fields = (new_mid_high, new_end_high, new_mid_low, new_end_low, strips, new_middle)
    mid, inner_sums = call(
        functools.partial(inner_kernel, True), "inner1", (PARTS[0], struct(2, DX, DY)), [VMEM] * 12, (VMEM,) * 2,
        **inner_cost,
    )(new_mid, *fields, move, gain, w, sums, table)
    end, ends = call(
        functools.partial(outer_kernel, True), "outer1", (PARTS[1], struct(2, DX, DY)), [VMEM] * 15, (VMEM,) * 2,
        **outer_cost,
    )(new_end, *fields, x_first, x_second, move, gain, w, sums, table, inner_sums)

    partner = lax.ppermute(ends, "gz", [(0, 1), (1, 0), (2, 3), (3, 2)])
    send, near = call(
        functools.partial(mix_kernel, mix), "mix", (struct(DX, DY), struct(2, DX, DY)), [VMEM, VMEM], (VMEM,) * 2,
    )(ends, partner)
    send, mid, end = lax.optimization_barrier((send, mid, end))
    far = lax.ppermute(send, "gz", [(0, 2), (2, 0), (1, 3), (3, 1)])
    swept = call(
        sweep_kernel, "sweep", struct(DZ, DX, DY), [VMEM, VMEM, SMEM], VMEM, [pltpu.VMEM((DZ, DX, DY), f32)],
        flops=20 << 20, nbytes=4 << 20,
    )(mid, end, solve)
    return call(
        functools.partial(finish_kernel, mix), "finish", struct(DZ, DX, DY), [VMEM] * 4, HBM,
        [pltpu.VMEM((DZ, DX, DY), f32), SEM((8,))], nbytes=6 << 20,
    )(swept, near, far, reply)


def solution(mesh):
    block = P("gz", "gx", "gy")
    in_specs = (block, block, block, P(), block, P(), P(), P())
    return jax.shard_map(local, mesh=mesh, in_specs=in_specs, out_specs=block, check_vma=False)
```

```python
import functools

import jax
import jax.numpy as jnp
import numpy as np
from jax import lax
from jax.experimental import pallas as pl
from jax.experimental.pallas import tpu as pltpu
from jax.sharding import PartitionSpec as P

DZ, DX, DY = 64, 32, 256
BONDS = 28
INNER = DX - 6
OUTER = [0, 1, 2, DX - 3, DX - 2, DX - 1]
f32, bf16 = jnp.float32, jnp.bfloat16
lateral_step = 0.02
dissolve_step = 0.25

VMEM = pl.BlockSpec(memory_space=pltpu.VMEM)
SMEM = pl.BlockSpec(memory_space=pltpu.SMEM)
HBM = pl.BlockSpec(memory_space=pltpu.HBM)
ANY = pl.BlockSpec(memory_space=pl.ANY)
SEM = pltpu.SemaphoreType.DMA


def call(kernel, name, out_shape, in_specs, out_specs, scratch=(), flops=0, nbytes=1 << 20, limit=16):
    return pl.pallas_call(
        kernel,
        name=name,
        out_shape=out_shape,
        in_specs=in_specs,
        out_specs=out_specs,
        scratch_shapes=list(scratch),
        cost_estimate=pl.CostEstimate(flops=flops, bytes_accessed=nbytes, transcendentals=0),
        compiler_params=pltpu.CompilerParams(vmem_limit_bytes=limit << 20),
    )


def struct(*dims, dtype=f32):
    return jax.ShapeDtypeStruct(dims, dtype)


PARTS = tuple(struct(n, DZ, DY, dtype=t) for t in (f32, bf16, bf16) for n in (INNER, 6))
PACK = struct(2, DZ, 128)
SLABS = struct(6 * DZ, 128)
TAIL = DZ // 4
WHOLE = struct(DX, DZ, DY)


def lanes():
    return lax.broadcasted_iota(jnp.int32, (DZ, 128), 1)


def at_lanes(pack, row, source, target, count):
    lane = lanes()
    moved = pltpu.roll(row, (target - source) % 128, 1)
    return jnp.where((lane >= target) & (lane < target + count), moved, pack)


def two_sides(left, right):
    return jnp.where(lanes() % 8 < 4, left, right)


def by_parity(axis, first, second):
    lane = lax.broadcasted_iota(jnp.int32, first.shape, 1)
    odd = lane < jnp.where(lax.axis_index(axis) % 2 == 1, 128, 0)
    return jnp.where(odd, first, second), jnp.where(odd, second, first)


def fold(strip, start):
    lane = lax.broadcasted_iota(jnp.int32, (TAIL, 128), 1)
    folded = jnp.zeros((TAIL, 128), f32)
    for part in range(4):
        moved = pltpu.roll(strip[TAIL * part : TAIL * part + TAIL], (32 * part - start) % 128, 1)
        folded = jnp.where(lane // 32 == part, moved, folded)
    return folded


def unfold(folded, start):
    return jnp.concatenate([pltpu.roll(folded, (start - 32 * part) % 128, 1) for part in range(4)], axis=0)


def slab(index):
    return pl.ds(DZ * index, DZ)


def tail(index):
    return pl.ds(6 * DZ + TAIL * index, TAIL)


def split(value):
    high = value.astype(bf16)
    return high, (value - high.astype(f32)).astype(bf16)


def add_middle(pack, row, x):
    slot = 8 * (x % 16)
    pack = at_lanes(pack, row[:, :128], 125, slot, 3)
    return at_lanes(pack, row[:, 128:], 0, slot + 4, 3)


def edge_window(before, after, x):
    slot = 8 * ((x + 13) % 16)
    lane = lanes()
    window = pltpu.roll(jnp.where(lane >= slot, before, after), (128 - slot) % 128, 1)
    high = window.astype(bf16).astype(f32)
    low = pltpu.roll(window - high, 64, 1)
    return jnp.concatenate([jnp.where(lane < 64, high, low).astype(bf16), high.astype(bf16)], axis=1)


def total_weight(weight):
    total = weight[0]
    for bond in range(1, BONDS):
        total = total + weight[bond]
    return total


def prepare_kernel(
    offsets_in, weight_in, diffusivity_in, rate_in, pit, phase, damage,
    w_ref, move, gain, table_rows, to_high, to_low,
    pv, hv, dv, offsets, weight, diffusivity, rate, table, sem, scalar_sem,
):
    def copies(group):
        return [
            pltpu.make_async_copy(source.at[:, x, :], target.at[x], sem.at[group])
            for x in range(8 * group, 8 * group + 8)
            for source, target in ((pit, pv), (phase, hv), (damage, dv))
        ]

    scalar_copies = [
        pltpu.make_async_copy(source, target, scalar_sem.at[i])
        for i, (source, target) in enumerate(
            ((offsets_in, offsets), (weight_in, weight), (diffusivity_in, diffusivity), (rate_in, rate))
        )
    ]
    for copy in scalar_copies:
        copy.start()
    for group in range(4):
        for copy in copies(group):
            copy.start()
    for copy in scalar_copies:
        copy.wait()
    for place in range(49):
        table[place] = jnp.float32(0.0)
    for bond in range(BONDS):
        place = (offsets[0, bond] + 3) * 7 + offsets[1, bond] + 3
        table[place] = table[place] + weight[bond]
    for place in range(49):
        table_rows[place : place + 1, :] = jnp.full((1, 128), table[place], f32)
    table_rows[49:50, :] = jnp.full((1, 128), total_weight(weight), f32)
    diff = lax.broadcasted_iota(jnp.int32, (128, 128), 0) - lax.broadcasted_iota(jnp.int32, (128, 128), 1) + 3
    blank = jnp.zeros((128, 128), bf16)
    for start in (0, 4):
        w_ref[start, :128, 128:] = blank
        w_ref[start + 3, 128:, :128] = blank
    for first in range(7):
        band = jnp.zeros((128, 128), f32)
        for second in range(7):
            band = jnp.where(diff == second, table[first * 7 + second], band)
        high, low = split(band)
        for out_row in range(2):
            row = first + out_row
            place = (slice(128 * (row % 2), 128 * (row % 2) + 128), slice(128 * out_row, 128 * out_row + 128))
            w_ref[(row // 2,) + place] = high
            w_ref[(4 + row // 2,) + place] = low
    lane = lax.broadcasted_iota(jnp.int32, (64, DY), 0)
    column = lax.broadcasted_iota(jnp.int32, (64, DY), 1)
    place = lane % 8
    first = lane // 8 - column // 128
    second = jnp.where(place < 4, place, 127 + place) - column % 128
    good = (place != 3) & (place != 7) & (first >= 0) & (first < 7) & (second >= 0) & (second < 7)
    which = jnp.where(good, 7 * first + second, -1)
    edge = jnp.zeros((64, DY), f32)
    for place in range(49):
        edge = jnp.where(which == place, table[place], edge)
    high, low = split(edge)
    for row, value in enumerate((high, high, low, jnp.zeros((64, DY), bf16))):
        w_ref[8, 64 * row : 64 * row + 64, :] = value
    def look(ids, values, scale):
        value = jnp.where(ids == 0, values[0] * scale, values[1] * scale)
        return jnp.where(ids < 2, value, jnp.where(ids == 2, values[2] * scale, values[3] * scale))

    for group in range(4):
        for copy in copies(group):
            copy.wait()

        @pl.loop(8 * group, 8 * group + 8)
        def _(x):
            ids = hv[x]
            move[x] = look(ids, diffusivity, lateral_step) * (1.0 + 0.5 * dv[x].astype(f32))
            gain[x] = look(ids, rate, dissolve_step) * pv[x].astype(f32)

        if group % 2 == 0:
            high, low = jnp.zeros((DZ, 128), f32), jnp.zeros((DZ, 128), f32)
        for x in range(8 * group, 8 * group + 8):
            slot = 8 * (x % 16)
            high = at_lanes(high, move[x, :, 128:], 125, slot, 3)
            high = at_lanes(high, gain[x, :, 128:], 125, slot + 4, 3)
            low = at_lanes(low, gain[x, :, :128], 0, slot, 3)
            low = at_lanes(low, move[x, :, :128], 0, slot + 4, 3)
        if group % 2:
            to_high[group // 2], to_low[group // 2] = by_parity("gy", high, low)


def right_side(w_ref):
    high, low = [w_ref[t] for t in range(4)], [w_ref[4 + t] for t in range(4)]
    return jnp.concatenate(high + high + low + [w_ref[8]], axis=0)


def pair_flux(pairs, high_of, low_of, edges, half, w_ref):
    part = slice(128 * half, 128 * half + 128)

    def side(row_of):
        return [jnp.concatenate([row_of(x - 3 + i)[:, part] for x in pairs], axis=0) for i in range(8)]

    high, low = side(high_of), side(low_of)
    left = jnp.concatenate(high + low + high + [edges], axis=1)
    flux = jnp.dot(left, right_side(w_ref), preferred_element_type=f32)

    def of(place, out_row):
        return flux[DZ * place : DZ * place + DZ, 128 * out_row : 128 * out_row + 128]

    return of


def stepped(center, flux, move, gain, weight_sum):
    return center + move * (flux - weight_sum * center) + gain * (1.0 - center)


def first_kernel(conc, mid, end, lasts, firsts, up, down, sem):
    def row_ref(x):
        return end.at[OUTER.index(x)] if x in OUTER else mid.at[x - 3]

    for x in range(DX):
        pltpu.make_async_copy(conc.at[:, x, :], row_ref(x), sem.at[x // 8]).start()
    for group in range(4):
        for x in range(8 * group, 8 * group + 8):
            pltpu.make_async_copy(conc.at[:, x, :], row_ref(x), sem.at[group]).wait()
        if group % 2 == 0:
            high_side, low_side = jnp.zeros((DZ, 128), f32), jnp.zeros((DZ, 128), f32)
        for x in range(8 * group, 8 * group + 8):
            slot = 8 * (x % 16)
            row = row_ref(x)
            high_side = at_lanes(high_side, row[:, 128:], 122, slot, 6)
            low_side = at_lanes(low_side, row[:, :128], 0, slot, 6)
        if group % 2:
            lasts[group // 2], firsts[group // 2] = by_parity("gy", high_side, low_side)
    fill_slabs(lambda row: end[row], up, down)


def fill_slabs(row_of, up, down):
    for row in range(3):
        for half in range(2):
            part = slice(128 * half, 128 * half + 128)
            place = slab(2 * row + half)
            up[place], down[place] = by_parity("gx", row_of(3 + row)[:, part], row_of(row)[:, part])


def join_kernel(y_first, y_second, own_first, own_second, up_in, down_in, strips, up, down):
    for group in range(2):
        right, left = by_parity("gy", y_first[group], y_second[group])
        lasts, firsts = by_parity("gy", own_first[group], own_second[group])
        strips[0, group] = two_sides(left, pltpu.roll(lasts, 1, 1))
        strips[1, group] = two_sides(pltpu.roll(left, 125, 1), pltpu.roll(right, 4, 1))
        strips[2, group] = two_sides(firsts, pltpu.roll(right, 1, 1))
    for index in range(6):
        up[slab(index)] = up_in[slab(index)]
        down[slab(index)] = down_in[slab(index)]
    for index in range(3):
        up[tail(index)], down[tail(index)] = by_parity("gx", fold(strips[index, 1], 96), fold(strips[index, 0], 0))


def strip_taps(table, first, second, third):
    place = lanes() % 4

    def moved(value, step):
        return pltpu.roll(value, step % 128, 1)

    columns = [
        first,
        jnp.where(place < 2, moved(first, -1), moved(second, 2)),
        jnp.where(place < 1, moved(first, -2), moved(second, 1)),
        second,
        jnp.where(place < 2, moved(second, -1), moved(third, 2)),
        jnp.where(place < 1, moved(second, -2), moved(third, 1)),
        third,
    ]
    sums = []
    for a in range(7):
        total = table[7 * a : 7 * a + 1, :] * columns[0]
        for second_index in range(1, 7):
            place = 7 * a + second_index
            total = total + table[place : place + 1, :] * columns[second_index]
        sums.append(total)
    return sums


def strip_flux(taps, group):
    lane = lanes()
    total = jnp.zeros((DZ, 128), f32)
    zero = jnp.zeros((DZ, 128), f32)
    for a in range(7):
        step = 8 * (a - 3)
        own, after, before = (
            zero if taps[g] is None else taps[g][a] for g in (group, (group + 1) % 3, (group + 2) % 3)
        )
        if step == 0:
            total = total + own
        elif step > 0:
            total = total + pltpu.roll(jnp.where(lane >= step, own, after), 128 - step, 1)
        else:
            total = total + pltpu.roll(jnp.where(lane < 128 + step, own, before), -step, 1)
    return total


def inner_kernel(last, mid, *rest):
    if last:
        mid_high, end_high, mid_low, end_low, strips, middle, move, gain, w_ref, sums, table, out, extra = rest
    else:
        (
            end, strips, move, gain, w_ref, table,
            out, out_high, out_low, extra, new_middle, mid_high, end_high, mid_low, end_low, middle,
        ) = rest
        packed = [jnp.zeros((DZ, 128), f32)] * 2
        for x in range(DX):
            if x in OUTER:
                place = OUTER.index(x)
                row = end[place]
                end_high[place], end_low[place] = split(row)
            else:
                row = mid[x - 3]
                mid_high[x - 3], mid_low[x - 3] = split(row)
            packed[x // 16] = add_middle(packed[x // 16], row, x)
        middle[0], middle[1] = packed
    halo = strips.at[0 if last else 1]
    weight_sum = table[49:50, :]
    pairs = range(3, DX - 3, 2)

    def row_of(mid_part, end_part):
        return lambda x: end_part[OUTER.index(x)] if x in OUTER else mid_part[x - 3]

    packed = [jnp.zeros((DZ, 128), f32)] * 2
    for half in range(2):
        around = [
            two_sides(halo[g], middle[g]) if half == 0 else two_sides(middle[g], halo[g]) for g in range(2)
        ]
        edges = []
        for x in pairs:
            group = (x + 13) // 16 - 1
            edges.append(edge_window(around[group], around[min(group + 1, 1)], x))
        flux = pair_flux(
            pairs, row_of(mid_high, end_high), row_of(mid_low, end_low), jnp.concatenate(edges, axis=0), half, w_ref
        )
        part = slice(128 * half, 128 * half + 128)
        for place, first in enumerate(pairs):
            for out_row in range(2):
                x = first + out_row
                row = x - 3
                new = stepped(mid[row, :, part], flux(place, out_row), move[x, :, part], gain[x, :, part], weight_sum)
                out[row, :, part] = new
                if not last:
                    out_high[row, :, part], out_low[row, :, part] = split(new)
                    slot = 8 * (x % 16)
                    source, target = (125, slot) if half == 0 else (0, slot + 4)
                    packed[x // 16] = at_lanes(packed[x // 16], new, source, target, 3)
    if last:
        extra[...] = jnp.zeros_like(extra)
        depth_sums(out, sums, extra, 3, INNER, 0)
    else:
        new_middle[0], new_middle[1] = packed
        taps = [strip_taps(table, strips[0, g], strips[1, g], strips[2, g]) for g in range(2)] + [None]
        for group in range(2):
            extra[group] = strip_flux(taps, group)


def depth_sums(rows, sums, extra, start, count, first):
    own = lax.axis_index("gz")
    for half in range(2):
        part = slice(128 * half, 128 * half + 128)
        below = jnp.zeros((count, 128), f32)
        above = jnp.zeros((count, 128), f32)
        for z in range(DZ):
            value = rows[first : first + count, z, part]
            below = below + sums[own, z : z + 1, :] * value
            above = above + sums[own, DZ + z : DZ + z + 1, :] * value
        extra[0, start : start + count, part] = below
        extra[1, start : start + count, part] = above


def outer_kernel(
    last, end, mid_high, end_high, mid_low, end_low, strips, middle, x_first, x_second, move, gain, w_ref,
    sums, table, extra_in, *rest,
):
    if last:
        out, extra = rest
    else:
        coefs_first, coefs_second, middle_in, out, out_high, out_low, extra, up, down, new_middle = rest
    halo = strips.at[0 if last else 1]
    weight_sum = table[49:50, :]
    zero = jnp.zeros((DZ, 128), f32)

    def halo_rows(slabs):
        return [jnp.concatenate([slabs[2 * row], slabs[2 * row + 1]], axis=1) for row in range(3)]

    def received(place):
        return by_parity("gx", x_first[place], x_second[place])

    from_high, from_low = zip(*(received(slab(index)) for index in range(6)))
    tails = [received(tail(index)) for index in range(1 if last else 3)]
    high_strips, low_strips = [unfold(high, 0) for high, _ in tails], [unfold(low, 96) for _, low in tails]
    low_rows, high_rows = halo_rows(from_low), halo_rows(from_high)
    low_split, high_split = [split(row) for row in low_rows], [split(row) for row in high_rows]
    low_middle, high_middle = zero, zero
    for row in range(3):
        low_middle = add_middle(low_middle, low_rows[row], 13 + row)
        high_middle = add_middle(high_middle, high_rows[row], row)
    here = 0 if last else 1
    sides = [low_strips[here], halo[0], halo[1], high_strips[here]]
    middles = [low_middle, middle[0], middle[1], high_middle]

    def row_of(which, mid_part, end_part):
        def of(x):
            if x < 0:
                return low_split[x + 3][which]
            if x >= DX:
                return high_split[x - DX][which]
            return end_part[OUTER.index(x)] if x in OUTER else mid_part[x - 3]

        return of

    pairs = [0, 2, DX - 4, DX - 2]
    packed = [zero, zero] if last else [middle_in[0], middle_in[1]]
    for half in range(2):
        around = [two_sides(p, q) if half == 0 else two_sides(q, p) for p, q in zip(sides, middles)]
        edges = []
        for x in pairs:
            group = (x + 13) // 16
            edges.append(edge_window(around[group], around[min(group + 1, 3)], x))
        flux = pair_flux(
            pairs, row_of(0, mid_high, end_high), row_of(1, mid_low, end_low), jnp.concatenate(edges, axis=0), half,
            w_ref,
        )
        part = slice(128 * half, 128 * half + 128)
        for row, x in enumerate(OUTER):
            place = [i for i in range(4) if pairs[i] <= x <= pairs[i] + 1][0]
            new = stepped(
                end[row, :, part], flux(place, x - pairs[place]), move[x, :, part], gain[x, :, part], weight_sum
            )
            out[row, :, part] = new
            if not last:
                out_high[row, :, part], out_low[row, :, part] = split(new)
                slot = 8 * (x % 16)
                source, target = (125, slot) if half == 0 else (0, slot + 4)
                packed[x // 16] = at_lanes(packed[x // 16], new, source, target, 3)
    if last:
        extra[...] = extra_in[...]
        depth_sums(out, sums, extra, 0, 3, 0)
        depth_sums(out, sums, extra, DX - 3, 3, 3)
    else:
        new_middle[0], new_middle[1] = packed
        fill_slabs(lambda row: out[row], up, down)
        lane = lanes()
        beyond = [jnp.where(lane < 64, high, low) for high, low in zip(high_strips, low_strips)]
        taps = [None, None, strip_taps(table, *beyond)]
        for group in range(2):
            flux = extra_in[group] + strip_flux(taps, group)
            right, left = by_parity("gy", coefs_first[group], coefs_second[group])
            extra[0, group] = stepped(
                halo[group], flux, two_sides(left, right),
                two_sides(pltpu.roll(left, 124, 1), pltpu.roll(right, 4, 1)), weight_sum,
            )
        up[tail(0)], down[tail(0)] = by_parity("gx", fold(extra[0, 1], 96), fold(extra[0, 0], 0))


def depth_tables():
    blocks = 4
    stiff = 3.0 * DZ * DZ
    count = DZ * blocks
    diagonal = np.full(count, 1.0 + 2.0 * stiff)
    diagonal[0] = diagonal[-1] = 1.0 + stiff
    fore = diagonal.copy()
    for i in range(1, count):
        fore[i] = diagonal[i] - stiff * stiff / fore[i - 1]
    back = diagonal.copy()
    for i in range(count - 2, -1, -1):
        back[i] = diagonal[i] - stiff * stiff / back[i + 1]

    def from_above(block, other):
        return np.prod(stiff / fore[other * DZ + DZ - 1 : block * DZ])

    def from_below(block, other):
        return np.prod(stiff / back[block * DZ + DZ : other * DZ + 1])

    sums = np.zeros((blocks, 2 * DZ))
    solve = np.zeros((blocks, 2 * DZ))
    reply = np.zeros((blocks, 2 * DZ))
    mix = np.zeros((blocks, 8))
    for block in range(blocks):
        start, end = block * DZ, block * DZ + DZ - 1
        pivots = fore[start : end + 1].copy()
        if block < blocks - 1:
            pivots[-1] = fore[end] - stiff * stiff / back[end + 1]
        for z in range(DZ):
            sums[block, z] = np.prod(stiff / fore[start + z : end])
            sums[block, DZ + z] = np.prod(stiff / back[start + 1 : start + z + 1])
            solve[block, z] = stiff / fore[start + z - 1] if z else 0.0
            solve[block, DZ + z] = 1.0 / pivots[z]
        for side, place in ((0, 0), (1, DZ - 1)):
            value = np.zeros(DZ)
            value[place] = 1.0
            for z in range(1, DZ):
                value[z] += solve[block, z] * value[z - 1]
            value[-1] /= pivots[-1]
            for z in range(DZ - 2, -1, -1):
                value[z] = (value[z] + stiff * value[z + 1]) / pivots[z]
            reply[block, side * DZ : side * DZ + DZ] = 2.0 * value
        partner = block ^ 1
        if block < 2:
            near, far = (1.0, from_above(3, 0) / from_above(3, 1))
            mix[block, 0:2] = (far, near) if block == 0 else (near, far)
            mix[block, 7] = from_below(block, 2)
        else:
            near, far = (1.0, from_below(0, 3) / from_below(0, 2))
            mix[block, 2:4] = (near, far) if block == 2 else (far, near)
            mix[block, 5] = from_above(block, 1)
        if partner < block:
            mix[block, 4] = from_above(block, partner)
        else:
            mix[block, 6] = from_below(block, partner)
    rows = [jnp.asarray(np.repeat(table[:, :, None], 128, axis=2), f32) for table in (sums, reply)]
    return rows[0], jnp.asarray(solve, f32), rows[1], mix


def own_of(mix, column):
    own = lax.axis_index("gz")
    value = jnp.float32(mix[0, column])
    for block in range(1, 4):
        value = jnp.where(own == block, jnp.float32(mix[block, column]), value)
    return value


def mix_kernel(mix, own_sums, partner_sums, send, near):
    send[...] = (
        own_of(mix, 0) * own_sums[0] + own_of(mix, 1) * partner_sums[0]
        + own_of(mix, 2) * own_sums[1] + own_of(mix, 3) * partner_sums[1]
    )
    near[0] = own_of(mix, 4) * partner_sums[0]
    near[1] = own_of(mix, 6) * partner_sums[1]


def sweep_kernel(mid, end, solve, sweep, buf):
    for row, x in enumerate(OUTER):
        buf[:, x, :] = end[row]
    for row in range(INNER):
        buf[:, 3 + row, :] = mid[row]
    own = lax.axis_index("gz")
    stiff = 3.0 * DZ * DZ
    value = buf[0]
    sweep[0] = value
    for z in range(1, DZ):
        value = buf[z] + solve[own, z] * value
        sweep[z] = value
    value = value * solve[own, 2 * DZ - 1]
    for z in range(DZ - 1, -1, -1):
        if z < DZ - 1:
            value = (sweep[z] + stiff * value) * solve[own, DZ + z]
        sweep[z] = 2.0 * value - buf[z]


def finish_kernel(mix, swept, near, far, reply, out, buf, out_sem):
    own = lax.axis_index("gz")
    above = near[0] + own_of(mix, 5) * far[...]
    below = near[1] + own_of(mix, 7) * far[...]
    size = 8

    def copy(z):
        part = pl.ds(z, size)
        return pltpu.make_async_copy(buf.at[part], out.at[part], out_sem.at[z // size])

    for start in range(0, DZ, size):
        for z in range(start, start + size):
            for half in range(2):
                part = slice(128 * half, 128 * half + 128)
                buf[z, :, part] = (
                    swept[z, :, part] + reply[own, z : z + 1, :] * above[:, part]
                    + reply[own, DZ + z : DZ + z + 1, :] * below[:, part]
                )
        copy(start).start()
    for start in range(0, DZ, size):
        copy(start).wait()


def swaps(first, second, axis):
    count = lax.axis_size(axis)
    moved = []
    for start, value in ((1, first), (0, second)):
        pairs = [(i, (i + 1) % count) for i in range(start, count, 2)]
        moved.append(lax.ppermute(value, axis, pairs + [(target, source) for source, target in pairs]))
    return moved


def local(conc, pit, phase, offsets, damage, weight, diffusivity, rate):
    sums, solve, reply, mix = depth_tables()
    mid, end, lasts, firsts, up, down = call(
        first_kernel, "first", PARTS[:2] + (PACK, PACK, SLABS, SLABS), [HBM], (VMEM,) * 6, [SEM((4,))],
        nbytes=4 << 20, limit=51,
    )(conc)
    left, right = swaps(lasts, firsts, "gy")
    w, move, gain, table, to_high, to_low = call(
        prepare_kernel, "prepare", (struct(9, DY, DY, dtype=bf16), WHOLE, WHOLE, struct(56, 128), PACK, PACK),
        [ANY] * 4 + [HBM] * 3, (VMEM,) * 6,
        [pltpu.VMEM((DX, DZ, DY), jnp.int32)] * 3
        + [pltpu.SMEM((2, BONDS), jnp.int32), pltpu.SMEM((BONDS,), f32), pltpu.SMEM((4,), f32), pltpu.SMEM((4,), f32)]
        + [pltpu.SMEM((64,), f32), SEM((4,)), SEM((4,))],
        nbytes=8 << 20, limit=47,
    )(offsets.T, weight, diffusivity, rate, pit, phase, damage)
    strips, up, down = call(
        join_kernel, "join", (struct(3, 2, DZ, 128), struct(6 * DZ + 3 * TAIL, 128), struct(6 * DZ + 3 * TAIL, 128)), [VMEM] * 6, (VMEM,) * 3,
    )(left, right, lasts, firsts, up, down)
    inner_cost = dict(flops=2 * INNER * DZ * DY * 3328, nbytes=12 << 20)
    outer_cost = dict(flops=2 * 8 * DZ * DY * 3328, nbytes=6 << 20)

    x_first, x_second = swaps(up, down, "gx")
    coefs = swaps(to_high, to_low, "gy")
    new_mid, new_mid_high, new_mid_low, flux, new_middle, mid_high, end_high, mid_low, end_low, middle = call(
        functools.partial(inner_kernel, False), "inner0",
        (PARTS[0], PARTS[2], PARTS[4], PACK, PACK, PARTS[2], PARTS[3], PARTS[4], PARTS[5], PACK),
        [VMEM] * 7, (VMEM,) * 10, **inner_cost,
    )(mid, end, strips, move, gain, w, table)
    new_end, new_end_high, new_end_low, strips, up, down, new_middle = call(
        functools.partial(outer_kernel, False), "outer0",
        (PARTS[1], PARTS[3], PARTS[5], struct(1, 2, DZ, 128), struct(6 * DZ + TAIL, 128), struct(6 * DZ + TAIL, 128), PACK),
        [VMEM] * 18, (VMEM,) * 7, **outer_cost,
    )(
        end, mid_high, end_high, mid_low, end_low, strips, middle, x_first, x_second, move, gain, w, sums, table, flux,
        *coefs, new_middle,
    )

    x_first, x_second = swaps(up, down, "gx")
    fields = (new_mid_high, new_end_high, new_mid_low, new_end_low, strips, new_middle)
    mid, inner_sums = call(
        functools.partial(inner_kernel, True), "inner1", (PARTS[0], struct(2, DX, DY)), [VMEM] * 12, (VMEM,) * 2,
        **inner_cost,
    )(new_mid, *fields, move, gain, w, sums, table)
    end, ends = call(
        functools.partial(outer_kernel, True), "outer1", (PARTS[1], struct(2, DX, DY)), [VMEM] * 15, (VMEM,) * 2,
        **outer_cost,
    )(new_end, *fields, x_first, x_second, move, gain, w, sums, table, inner_sums)

    partner = lax.ppermute(ends, "gz", [(0, 1), (1, 0), (2, 3), (3, 2)])
    send, near = call(
        functools.partial(mix_kernel, mix), "mix", (struct(DX, DY), struct(2, DX, DY)), [VMEM, VMEM], (VMEM,) * 2,
    )(ends, partner)
    send, mid, end = lax.optimization_barrier((send, mid, end))
    far = lax.ppermute(send, "gz", [(0, 2), (2, 0), (1, 3), (3, 1)])
    swept = call(
        sweep_kernel, "sweep", struct(DZ, DX, DY), [VMEM, VMEM, SMEM], VMEM, [pltpu.VMEM((DZ, DX, DY), f32)],
        flops=20 << 20, nbytes=4 << 20,
    )(mid, end, solve)
    return call(
        functools.partial(finish_kernel, mix), "finish", struct(DZ, DX, DY), [VMEM] * 4, HBM,
        [pltpu.VMEM((DZ, DX, DY), f32), SEM((8,))], nbytes=6 << 20,
    )(swept, near, far, reply)


def solution(mesh):
    block = P("gz", "gx", "gy")
    in_specs = (block, block, block, P(), block, P(), P(), P())
    return jax.shard_map(local, mesh=mesh, in_specs=in_specs, out_specs=block, check_vma=False)
```
